512 devices in a mesh: seq: 64 (over x, y, z_lo), tp: 8 (over z_hi, core).
Axes of the slice: x: 4, y: 8, z: 8 (z_hi: 4, z_lo: 2; z = z_hi * 2 + z_lo), core: 2. Of those that a mesh axis runs over, the one named last changes fastest.
Arguments:
- hidden_in: bfloat16 [16384, 2048], P('seq', 'tp'), may hold values from -6 to 6
- norm_gain: float32 [2048], replicated, may hold values from 0.1 to 1.9
- norm_bias: float32 [2048], replicated, may hold values from -3 to 3
- qkv_weight: bfloat16 [3, 2048, 2048], P(None, 'seq', 'tp'), may hold values from -0.125 to 0.125
- qkv_bias: float32 [3, 2048], P(None, 'tp'), may hold values from -3 to 3
- out_weight: bfloat16 [2048, 2048], P('tp', 'seq'), may hold values from -0.125 to 0.125
- out_bias: float32 [2048], P('tp'), may hold values from -3 to 3
- key_cache: bfloat16 [147456, 2048], P('seq', 'tp')
- value_cache: bfloat16 [147456, 2048], P('seq', 'tp'), may hold values from -6 to 6
- cached_len: int32 [16], replicated, may hold values from 0 to 8192, as said below
Outputs:
- mixed: bfloat16 [16384, 2048], P('seq', 'tp')
- key_cache_new: bfloat16 [147456, 2048], P('seq', 'tp')
- value_cache_new: bfloat16 [147456, 2048], P('seq', 'tp')
The draws below stay inside these ranges and needn't reach their ends.
Inputs may be any that keep to these rules, and one draw needn't show every extreme that they name: `cached_len`: some request has exactly 8192 cached positions.
All inputs are finite; a program needn't handle non-finite values.
Results may differ from the reference program's by a relative error of at most 0.035.
Values may be sent and summed in bfloat16 or wider, within the bound.
A program may use at most 64 MiB of HBM per device.

```python
import math
import jax
import jax.numpy as jnp
from jax import lax

D = 2048
HEADS = 16
HEAD_DIM = 128
REQS = 16
SPAN = 1024
MAXLEN = 8192
TOKENS = 16384
CAP = 9216


def draw_key_cache(key, part):
    first_key = jax.random.fold_in(jax.random.fold_in(key, 11), 0)
    base = jax.random.normal(first_key, (REQS * CAP, D), jnp.float32)
    base = jnp.clip(base, -6.0, 6.0)
    return base.astype(jnp.bfloat16)


def draw_cached_len(key, part):
    first_key, second_key = jax.random.split(jax.random.fold_in(key, 23))
    lengths = jax.random.randint(first_key, (REQS,), 0, MAXLEN + 1)
    chosen = jax.random.randint(second_key, (), 0, REQS)
    return jnp.where(jnp.arange(REQS) == chosen, MAXLEN, lengths).astype(jnp.int32)


def block_levels(key, dims, pieces, least, top_value):
    factor_of, own = 1.0, jax.random.fold_in(key, 6)
    for axis_at, parts in pieces:
        steps = jnp.exp(jax.random.uniform(jax.random.fold_in(own, axis_at), (parts,), jnp.float32, least / len(pieces), top_value / len(pieces)))
        factor_of = factor_of * jnp.repeat(steps, dims[axis_at] // parts).reshape([-1 if axis == axis_at else 1 for axis in range(len(dims))])
    return factor_of


def gaussian(rng, extent, spread, most, pieces=(), dtype=jnp.bfloat16):
    values = jax.random.normal(rng, extent, jnp.float32) * spread
    if len(pieces) > 0:
        values = block_levels(rng, extent, pieces, -0.22, 0.18) * values
    return jnp.clip(values, min=-most, max=most).astype(dtype)


def setup_inputs(seed: int = 0) -> dict:
    keys = jax.random.split(jax.random.key(seed), 11)
    hidden_in = gaussian(keys[0], (TOKENS, D), 1.0, 6.0, ((0, 64), (1, 8)))
    norm_gain = jnp.clip(1.0 + 0.18 * jax.random.normal(keys[1], (D,), jnp.float32), 0.1, 1.9)
    norm_bias = gaussian(keys[2], (D,), 0.5, 3.0, (), jnp.float32)
    qkv_weight = gaussian(keys[3], (3, D, D), D ** -0.5, 0.125, ((1, 64), (2, 8)))
    qkv_bias = gaussian(keys[4], (3, D), 0.5, 3.0, ((1, 8),), jnp.float32)
    out_weight = gaussian(keys[5], (D, D), D ** -0.5, 0.125, ((0, 8), (1, 64)))
    out_bias = gaussian(keys[6], (D,), 0.5, 3.0, ((0, 8),), jnp.float32)
    key_cache = draw_key_cache(jax.random.fold_in(keys[10], 71), 0)
    value_cache = gaussian(keys[8], (REQS * CAP, D), 1.0, 6.0, ((0, 64), (1, 8)))
    cached_len = draw_cached_len(jax.random.fold_in(keys[10], 71), 0)
    return dict(hidden_in=hidden_in, norm_gain=norm_gain, norm_bias=norm_bias, qkv_weight=qkv_weight, qkv_bias=qkv_bias, out_weight=out_weight, out_bias=out_bias, key_cache=key_cache, value_cache=value_cache, cached_len=cached_len)


def reference(hidden_in, norm_gain, norm_bias, qkv_weight, qkv_bias, out_weight, out_bias, key_cache, value_cache, cached_len):
    values_f = hidden_in.astype(jnp.float32)
    row_mean = lax.optimization_barrier(jnp.mean(values_f, axis=-1, keepdims=True))
    row_var = lax.optimization_barrier(jnp.mean(jnp.square(values_f - row_mean), axis=-1, keepdims=True))
    normed = ((values_f - row_mean) * lax.rsqrt(row_var + 1e-05) * norm_gain + norm_bias).astype(jnp.bfloat16)
    projected = [(jnp.dot(normed, qkv_weight[index], preferred_element_type=jnp.float32) + qkv_bias[index]).astype(jnp.bfloat16) for index in range(3)]
    queries, fresh_keys, fresh_values = projected
    slopes = jnp.exp2(-8.0 * (jnp.arange(HEADS) + 1).astype(jnp.float32) / HEADS)
    key_pos = jnp.arange(CAP)
    key_all = key_cache.reshape(REQS, CAP, D)
    value_all = value_cache.reshape(REQS, CAP, D)
    keys_out = []
    values_out = []
    attended = []
    for request in range(REQS):
        length = cached_len[request].astype(jnp.int32)
        first_row = request * SPAN
        keys_req = lax.dynamic_update_slice(key_all[request], fresh_keys[first_row:first_row + SPAN], (length, jnp.int32(0)))
        values_req = lax.dynamic_update_slice(value_all[request], fresh_values[first_row:first_row + SPAN], (length, jnp.int32(0)))
        keys_out.append(keys_req)
        values_out.append(values_req)
        query_pos = length + jnp.arange(SPAN)
        distance = (query_pos[:, None] - key_pos[None, :]).astype(jnp.float32)
        valid = distance >= 0.0
        query_heads = queries[first_row:first_row + SPAN].reshape(SPAN, HEADS, HEAD_DIM).transpose(1, 0, 2)
        key_heads = keys_req.reshape(CAP, HEADS, HEAD_DIM).transpose(1, 0, 2)
        value_heads = values_req.reshape(CAP, HEADS, HEAD_DIM).transpose(1, 0, 2)

        def one_head(item):
            query_one, key_one, value_one, slope = item
            scores = jnp.dot(query_one, key_one.T, preferred_element_type=jnp.float32) / math.sqrt(HEAD_DIM) - slope * distance
            top_score = lax.optimization_barrier(jnp.max(jnp.where(valid, scores, -1e+30), axis=1, keepdims=True))
            weights = jnp.where(valid, jnp.exp(scores - top_score), 0.0)
            totals = lax.optimization_barrier(jnp.sum(weights, axis=1, keepdims=True))
            summed = jnp.dot(weights.astype(jnp.bfloat16), value_one, preferred_element_type=jnp.float32)
            return summed / totals
        heads_out = lax.map(one_head, (query_heads, key_heads, value_heads, slopes))
        attended.append(heads_out.transpose(1, 0, 2).reshape(SPAN, D).astype(jnp.bfloat16))
    attended_all = jnp.concatenate(attended, axis=0)
    mixed = (jnp.dot(attended_all, out_weight, preferred_element_type=jnp.float32) + out_bias).astype(jnp.bfloat16)
    return (mixed, jnp.concatenate(keys_out, axis=0), jnp.concatenate(values_out, axis=0))
```

```python
import functools
import math

import jax
import jax.numpy as jnp
import numpy as np
from jax import lax
from jax.experimental import pallas as pl
from jax.experimental.pallas import tpu as pltpu
from jax.sharding import PartitionSpec as P

HEADS = 16
HEAD_DIM = 128
REQS = 16
SPAN = 1024
NX, NY, NZ = 4, 8, 2
TP = 8
ROWS = 256
SLOTS = 2304
LOG2E = 1.4426950408889634
MESH = pl.DeviceIdType.MESH
BF16 = jnp.bfloat16
F32 = jnp.float32
VMEM_SPEC = pl.BlockSpec(memory_space=pltpu.VMEM)
SMEM_SPEC = pl.BlockSpec(memory_space=pltpu.SMEM)


class Node:
    def __init__(self, tree, ox, oy, way, parent):
        self.tree, self.ox, self.oy, self.way, self.parent = tree, ox, oy, way, parent
        self.depth = 0 if parent is None else parent.depth + 1
        self.kids = []
        self.sem = None
        if parent is not None:
            parent.kids.append(self)


def build_tree(tree):
    root = Node(tree, 0, 0, None, None)

    def ring(start, axis, far_up):
        size = (NX, NY)[axis]
        for sign in (1, -1):
            most = size // 2 - (0 if (sign == 1) == far_up else 1)
            node = start
            for _ in range(most):
                step = [0, 0]
                step[axis] = -sign
                node = Node(tree, node.ox + step[0], node.oy + step[1], (axis, sign), node)
                yield node

    first, second = (0, 1) if tree == 0 else (1, 0)
    nodes = [root] + list(ring(root, first, True))
    flip = {}
    for node in list(nodes):
        off = node.ox if first == 0 else node.oy
        nodes += list(ring(node, second, (off % 2 == 0) if first == 1 else off in (0, -1)))
    return nodes


TREES = [build_tree(0), build_tree(1)]
EDGES = []
for _tree in TREES:
    for _node in _tree:
        if _node.parent is not None:
            _node.sem = len(EDGES)
            EDGES.append(_node)
N_EDGES = len(EDGES)
ORDER = sorted(EDGES, key=lambda n: (n.depth, n.sem))


class Place:
    def __init__(self):
        self.s = lax.axis_index("seq")
        self.t = lax.axis_index("tp")
        self.x = lax.div(self.s, NY * NZ)
        self.y = lax.rem(lax.div(self.s, NZ), NY)
        self.z = lax.rem(self.s, NZ)
        self.zh = lax.div(self.t, 2)
        self.core = lax.rem(self.t, 2)

    def seq(self, x, y, z):
        return (x * NY + y) * NZ + z

    def beside(self, axis, sign):
        if axis == 0:
            return (self.seq(lax.rem(self.x + sign + NX, NX), self.y, self.z), self.t)
        return (self.seq(self.x, lax.rem(self.y + sign + NY, NY), self.z), self.t)

    def z_partner(self):
        return (self.seq(self.x, self.y, 1 - self.z), self.t)

    def y_partner(self):
        return (self.seq(self.x, self.y + 1 - 2 * lax.rem(self.y, 2), self.z), self.t)

    def diagonal(self):
        return (self.seq(self.x, self.y + 1 - 2 * lax.rem(self.y, 2), 1 - self.z), self.t)

    def core_partner(self):
        return (self.s, self.zh * 2 + 1 - self.core)

    def up(self, hops):
        return (self.s, lax.rem(self.zh + hops + 4, 4) * 2 + self.core)

    def piece(self, bufs, node):
        ax = lax.rem(self.x + node.ox + NX, NX)
        ay = lax.rem(self.y + node.oy + NY, NY)
        if node.tree == 0:
            return bufs[0].at[ay, ax]
        return bufs[1].at[ax, ay]


def greet(devices):
    barrier = pltpu.get_barrier_semaphore()
    for device in devices:
        pl.semaphore_signal(barrier, inc=1, device_id=device, device_id_type=MESH)
    pl.semaphore_wait(barrier, len(devices))


def remote(src, dst, send_sem, recv_sem, device):
    return pltpu.make_async_remote_copy(
        src_ref=src, dst_ref=dst, send_sem=send_sem, recv_sem=recv_sem,
        device_id=device, device_id_type=MESH,
    )


class Gather:
    def __init__(self, place, halves, bufs, local_sem, zsend, zrecv, send, recv):
        self.p, self.halves, self.bufs = place, halves, bufs
        self.local_sem, self.zsend, self.zrecv, self.send, self.recv = local_sem, zsend, zrecv, send, recv
        self.sent = []

    def own(self, k):
        p = self.p
        return self.bufs[0].at[p.y, p.x, p.z] if k == 0 else self.bufs[1].at[p.x, p.y, p.z]

    def other(self, k):
        p = self.p
        return self.bufs[0].at[p.y, p.x, 1 - p.z] if k == 0 else self.bufs[1].at[p.x, p.y, 1 - p.z]

    def begin(self):
        self.locals = []
        for k in (0, 1):
            copy = remote(self.halves[k], self.own(k), self.zsend.at[k], self.zrecv.at[k], self.p.z_partner())
            copy.start()
            self.sent.append(copy)
        for k in (0, 1):
            copy = pltpu.make_async_copy(self.halves[k], self.own(k), self.local_sem.at[k])
            copy.start()
            self.locals.append(copy)

    def forward(self, node):
        for kid in node.kids:
            piece = self.p.piece(self.bufs, node)
            copy = remote(piece, piece, self.send.at[kid.sem], self.recv.at[kid.sem], self.p.beside(*kid.way))
            copy.start()
            self.sent.append(copy)

    def roots(self):
        for k in (0, 1):
            self.locals[k].wait()
            other = self.other(k)
            remote(other, other, self.zsend.at[k], self.zrecv.at[k], self.p.z_partner()).wait_recv()
            self.forward(TREES[k][0])

    def take(self, node):
        piece = self.p.piece(self.bufs, node)
        way = (node.way[0], -node.way[1])
        remote(piece, piece, self.send.at[node.sem], self.recv.at[node.sem], self.p.beside(*way)).wait_recv()
        self.forward(node)

    def finish(self):
        for copy in self.sent:
            copy.wait_send()


class TpGather:
    def __init__(self, place, src, buf, local_sem, send, recv):
        self.p, self.src, self.buf = place, src, buf
        self.local_sem, self.send, self.recv = local_sem, send, recv
        self.sent = []

    def block(self, hops, mine=True):
        p = self.p
        core = p.core if mine else 1 - p.core
        return self.buf.at[lax.rem(p.zh + hops + 4, 4) * 2 + core]

    def copy(self, src, dst, index, device):
        return remote(src, dst, self.send.at[index], self.recv.at[index], device)

    def start(self, src, dst, index, device):
        copy = self.copy(src, dst, index, device)
        copy.start()
        self.sent.append(copy)

    def begin(self):
        p = self.p
        self.start(self.src, self.block(0), 0, p.up(1))
        self.start(self.src, self.block(0), 1, p.up(-1))
        self.start(self.src, self.block(0), 4, p.core_partner())
        self.local = pltpu.make_async_copy(self.src, self.block(0), self.local_sem)
        self.local.start()

    def near(self):
        p = self.p
        half = ROWS // 2
        low, high = self.block(-1), self.block(1)
        self.copy(low, low, 0, p.up(-1)).wait_recv()
        self.start(low.at[pl.ds(0, half)], low.at[pl.ds(0, half)], 2, p.up(1))
        self.start(low, low, 5, p.core_partner())
        self.copy(high, high, 1, p.up(1)).wait_recv()
        self.start(high.at[pl.ds(half, half)], high.at[pl.ds(half, half)], 3, p.up(-1))
        self.start(high, high, 6, p.core_partner())

    def far(self):
        p = self.p
        half = ROWS // 2
        block = self.block(2)
        lower, upper = block.at[pl.ds(0, half)], block.at[pl.ds(half, half)]
        self.copy(lower, lower, 2, p.up(-1)).wait_recv()
        self.copy(upper, upper, 3, p.up(1)).wait_recv()
        self.start(block, block, 7, p.core_partner())

    def rest(self):
        self.local.wait()
        for index, hops in ((4, 0), (5, -1), (6, 1), (7, 2)):
            block = self.block(hops, mine=False)
            self.copy(block, block, index, self.p.core_partner()).wait_recv()

    def finish(self):
        for copy in self.sent:
            copy.wait_send()


def weight_rows(a_ref, b_ref, seqs, pick):
    parts = []
    for s in seqs:
        x, y, z = s // (NY * NZ), (s // NZ) % NY, s % NZ
        parts.append(a_ref[(y, x, z) + pick])
        parts.append(b_ref[(x, y, z) + pick])
    return jnp.concatenate(parts, axis=0)


def project_kernel(
    hidden_ref, gain_ref, shift_ref, weight_ref, bias_ref, out_ref,
    hid, wa, wb, norm,
    local_sem, zsend, zrecv, send, recv, hsend, hrecv,
):
    p = Place()
    greet([p.z_partner(), p.core_partner(), p.up(1), p.up(-1),
           p.beside(0, 1), p.beside(0, -1), p.beside(1, 1), p.beside(1, -1)])
    half = weight_ref.shape[1] // 2
    halves = [weight_ref.at[:, pl.ds(0, half)], weight_ref.at[:, pl.ds(half, half)]]
    weights = Gather(p, halves, (wa, wb), local_sem, zsend, zrecv, send, recv)
    tokens = TpGather(p, hidden_ref, hid, local_sem.at[2], hsend, hrecv)
    weights.begin()
    tokens.begin()
    weights.roots()

    def normalise(first, rows):
        values = [hid[t, first:first + rows, :].astype(F32) for t in range(TP)]
        total = functools.reduce(jnp.add, values)
        mean = jnp.sum(total, axis=1, keepdims=True) * (1.0 / (TP * ROWS))
        values = [v - mean for v in values]
        squares = functools.reduce(jnp.add, [v * v for v in values])
        variance = jnp.sum(squares, axis=1, keepdims=True) * (1.0 / (TP * ROWS))
        scale = lax.rsqrt(variance + 1e-05)
        for t in range(TP):
            norm[t, first:first + rows, :] = (values[t] * scale * gain_ref[t] + shift_ref[t]).astype(BF16)

    depth = 0
    for node in ORDER:
        if node.depth != depth:
            depth = node.depth
            if depth == 2:
                tokens.near()
            elif depth == 3:
                tokens.far()
            elif depth == 4:
                tokens.rest()
            elif depth == 5:
                normalise(0, 128)
            elif depth == 6:
                normalise(128, 128)
        weights.take(node)
    for index in range(3):
        total = None
        for t in range(TP):
            rows = weight_rows(wa, wb, range(t * 8, t * 8 + 8), (index,))
            part = jnp.dot(norm[t], rows, preferred_element_type=F32)
            total = part if total is None else total + part
        total = total + bias_ref[index]
        if index == 0:
            total = total * (LOG2E / math.sqrt(HEAD_DIM))
        out_ref[index] = total.astype(BF16)
    weights.finish()
    tokens.finish()


def share_kernel(
    qkv_ref, out_weight_ref, all_ref, oa_ref, ob_ref,
    local_sem, zsend, zrecv, send, recv, gsend, grecv,
):
    p = Place()
    greet([p.z_partner(), p.y_partner(), p.diagonal(),
           p.beside(0, 1), p.beside(0, -1), p.beside(1, 1), p.beside(1, -1)])
    half = out_weight_ref.shape[0] // 2
    halves = [out_weight_ref.at[pl.ds(0, half)], out_weight_ref.at[pl.ds(half, half)]]
    weights = Gather(p, halves, (oa_ref, ob_ref), local_sem, zsend, zrecv, send, recv)
    local = lax.rem(p.s, 4)
    slot = all_ref.at[local]
    sent = []
    peers = [p.y_partner(), p.z_partner(), p.diagonal()]
    for index, peer in enumerate(peers):
        copy = remote(qkv_ref, slot, gsend.at[index], grecv.at[index], peer)
        copy.start()
        sent.append(copy)
    weights.begin()
    mine = pltpu.make_async_copy(qkv_ref, slot, local_sem.at[2])
    mine.start()
    weights.roots()
    for node in ORDER:
        weights.take(node)
    for index, peer in enumerate(peers):
        theirs = all_ref.at[lax.rem(peer[0], 4)]
        remote(theirs, theirs, gsend.at[index], grecv.at[index], peer).wait_recv()
    mine.wait()
    weights.finish()
    for copy in sent:
        copy.wait_send()


def attend_kernel(
    numbers_ref, q_ref, keys_ref, values_ref, fresh_ref, bias_ref, out_ref, lse_ref, kaug, vaug,
):
    block = pl.program_id(0)
    first, local = numbers_ref[0], numbers_ref[1]

    @pl.when(block == 0)
    def _():
        def aux(count, start, live_only):
            place = lax.broadcasted_iota(jnp.int32, (count, HEAD_DIM), 0) + start
            lane = lax.broadcasted_iota(jnp.int32, (count, HEAD_DIM), 1)
            high = lax.shift_right_arithmetic(place, 7)
            low = place - high * 128
            number = jnp.where(lane < 3, high, jnp.where(lane < 6, low, 0)).astype(F32)
            if live_only:
                dead = place >= 0
                number = jnp.where(dead, jnp.where(lane == 6, -1e30, 0.0), number)
            return number.astype(BF16)

        cached = aux(SLOTS, first, True)
        fresh = aux(ROWS, local * ROWS, False)
        alive = lax.broadcasted_iota(jnp.int32, (SLOTS, HEAD_DIM), 0) + first < 0
        one = lax.broadcasted_iota(jnp.int32, (SLOTS, HEAD_DIM), 1) == 0
        ones = jnp.where(one, 1.0, 0.0).astype(BF16)
        for head in range(2):
            cols = slice(head * HEAD_DIM, (head + 1) * HEAD_DIM)
            kaug[head, :SLOTS, :HEAD_DIM] = jnp.where(alive, keys_ref[:, cols].astype(F32), 0.0).astype(BF16)
            kaug[head, :SLOTS, HEAD_DIM:] = cached
            kaug[head, SLOTS:, :HEAD_DIM] = fresh_ref[1, :, cols]
            kaug[head, SLOTS:, HEAD_DIM:] = fresh
            vaug[head, :SLOTS, :HEAD_DIM] = values_ref[:, cols]
            vaug[head, :SLOTS, HEAD_DIM:] = ones
            vaug[head, SLOTS:, :HEAD_DIM] = fresh_ref[2, :, cols]
            vaug[head, SLOTS:, HEAD_DIM:] = ones[:ROWS]

    row = lax.broadcasted_iota(jnp.int32, (ROWS, ROWS), 0) + block * ROWS
    column = lax.broadcasted_iota(jnp.int32, (ROWS, ROWS), 1) + local * ROWS
    lses = []
    for head in range(2):
        cols = slice(head * HEAD_DIM, (head + 1) * HEAD_DIM)
        bias = jnp.broadcast_to(bias_ref[head].astype(F32), (ROWS, HEAD_DIM)).astype(BF16)
        query = jnp.concatenate([q_ref[0, 0, :, cols], bias], axis=1)
        nt = (((1,), (1,)), ((), ()))
        cached = lax.dot_general(query, kaug[head, :SLOTS], nt, preferred_element_type=F32)
        fresh = lax.dot_general(query, kaug[head, SLOTS:], nt, preferred_element_type=F32)
        fresh = jnp.where(column <= row, fresh, -1e30)
        top = jnp.maximum(
            jnp.max(cached, axis=1, keepdims=True), jnp.max(fresh, axis=1, keepdims=True)
        )
        weight_c = jnp.exp2(cached - top).astype(BF16)
        weight_f = jnp.exp2(fresh - top).astype(BF16)
        both = jnp.dot(weight_c, vaug[head, :SLOTS], preferred_element_type=F32)
        both += jnp.dot(weight_f, vaug[head, SLOTS:], preferred_element_type=F32)
        total = both[:, HEAD_DIM:HEAD_DIM + 1]
        out_ref[0, :, cols] = (both[:, :HEAD_DIM] / total).astype(BF16)
        lses.append(top + jnp.log2(total))
    lane = lax.broadcasted_iota(jnp.int32, (ROWS, HEAD_DIM), 1)
    side = jnp.where(lane == 0, lses[0], lses[1])
    lse_ref[0] = jnp.transpose(side)[:8]


def output_kernel(
    part_ref, lse_ref, oa_ref, ob_ref, bias_ref, out_ref,
    parts, sides, mine, att, local_sem, psend, precv, tsend, trecv,
):
    p = Place()
    peers = [p.y_partner(), p.z_partner(), p.diagonal()]
    greet(peers + [p.core_partner(), p.up(1), p.up(-1)])
    local = lax.rem(p.s, 4)
    sent = []
    for index, peer in enumerate(peers):
        theirs = lax.rem(peer[0], 4)
        for copy in (
            remote(part_ref.at[theirs], parts.at[local], psend.at[index], precv.at[index], peer),
            remote(lse_ref.at[theirs], sides.at[local], psend.at[3 + index], precv.at[3 + index], peer),
        ):
            copy.start()
            sent.append(copy)
    own = [
        pltpu.make_async_copy(part_ref.at[local], parts.at[local], local_sem.at[1]),
        pltpu.make_async_copy(lse_ref.at[local], sides.at[local], local_sem.at[2]),
    ]
    for copy in own:
        copy.start()
    for copy in own:
        copy.wait()
    for index, peer in enumerate(peers):
        theirs = lax.rem(peer[0], 4)
        a, b = parts.at[theirs], sides.at[theirs]
        remote(a, a, psend.at[index], precv.at[index], peer).wait_recv()
        remote(b, b, psend.at[3 + index], precv.at[3 + index], peer).wait_recv()
    stats = [sides[k] for k in range(4)]
    top = functools.reduce(jnp.maximum, stats)
    shares = [jnp.exp2(stat - top) for stat in stats]
    total = functools.reduce(jnp.add, shares)
    shares = [jnp.transpose(jnp.concatenate([share / total] * 16, axis=0)) for share in shares]
    for head in range(2):
        cols = slice(head * HEAD_DIM, (head + 1) * HEAD_DIM)
        terms = [parts[k, :, cols].astype(F32) * shares[k][:, head:head + 1] for k in range(4)]
        mine[:, cols] = functools.reduce(jnp.add, terms).astype(BF16)
    gather = TpGather(p, mine, att, local_sem.at[0], tsend, trecv)
    gather.begin()
    gather.near()
    gather.far()
    gather.rest()
    result = None
    for t in range(TP):
        rows = weight_rows(oa_ref, ob_ref, range(t, 64, TP), ())
        term = lax.dot_general(att[t], rows, (((1,), (1,)), ((), ())), preferred_element_type=F32)
        result = term if result is None else result + term
    out_ref[...] = (result + bias_ref[...]).astype(BF16)
    gather.finish()
    for copy in sent:
        copy.wait_send()


PAD = ROWS + 32


def cache_kernel(numbers_ref, all_ref, keys_ref, values_ref, keys_out, values_out, fresh):
    step = pl.program_id(0)

    @pl.when(step == 0)
    def _():
        for k in range(2):
            for h in range(2):
                fresh[2 * k + h, :PAD] = jnp.zeros((PAD, HEAD_DIM), F32)
                fresh[2 * k + h, PAD + SPAN:] = jnp.zeros((PAD, HEAD_DIM), F32)
                for block in range(4):
                    rows = all_ref[block, 1 + k, :, h * HEAD_DIM:(h + 1) * HEAD_DIM]
                    fresh[2 * k + h, PAD + block * ROWS:PAD + (block + 1) * ROWS] = rows.astype(F32)

    start = step * ROWS + numbers_ref[0]
    touched = (start > -ROWS) & (start < SPAN)

    @pl.when(touched)
    def _():
        begin = jnp.clip(start, -ROWS, SPAN)
        place = lax.broadcasted_iota(jnp.int32, (ROWS, HEAD_DIM), 0) + begin
        inside = (place >= 0) & (place < SPAN)
        for k, (old, new) in enumerate(((keys_ref, keys_out), (values_ref, values_out))):
            for h in range(2):
                cols = slice(h * HEAD_DIM, (h + 1) * HEAD_DIM)
                rows = fresh[2 * k + h, pl.ds(begin + PAD, ROWS), :]
                new[:, cols] = jnp.where(inside, rows, old[:, cols].astype(F32)).astype(BF16)

    @pl.when(jnp.logical_not(touched))
    def _():
        keys_out[...] = keys_ref[...]
        values_out[...] = values_ref[...]


def round_bf16(value):
    return np.asarray(np.asarray(value, np.float32).astype(jnp.bfloat16), np.float64)


def bias_table():
    table = np.zeros((HEADS, 1, HEAD_DIM), np.float64)
    for head in range(HEADS):
        slope = 2.0 ** (-8.0 * (head + 1) / HEADS) * LOG2E
        for column, value in ((0, slope * 128.0), (3, slope)):
            rest = value
            for k in range(3):
                table[head, 0, column + k] = round_bf16(rest)
                rest = rest - table[head, 0, column + k]
        table[head, 0, 6] = 1.0
    return table.astype(np.float32)


def remote_params(ident):
    return pltpu.CompilerParams(collective_id=ident, has_side_effects=True, vmem_limit_bytes=48 << 20)


def dma(*count):
    return pltpu.SemaphoreType.DMA(count)


def on_device(
    hidden_in, norm_gain, norm_bias, qkv_weight, qkv_bias, out_weight, out_bias, key_cache, value_cache, cached_len,
):
    moves = []
    for s in range(64):
        for t in range(TP):
            moves.append((s * TP + t, ((s % 8) * 8 + t) * TP + s // 8))
    out_block = lax.ppermute(out_weight.T, ("seq", "tp"), moves)

    qkv = pl.pallas_call(
        project_kernel,
        name="project",
        out_shape=jax.ShapeDtypeStruct((3, ROWS, ROWS), BF16),
        in_specs=[VMEM_SPEC] * 5,
        out_specs=VMEM_SPEC,
        scratch_shapes=[
            pltpu.VMEM((TP, ROWS, ROWS), BF16),
            pltpu.VMEM((NY, NX, NZ, 3, 16, ROWS), BF16),
            pltpu.VMEM((NX, NY, NZ, 3, 16, ROWS), BF16),
            pltpu.VMEM((TP, ROWS, ROWS), BF16),
            dma(3), dma(2), dma(2), dma(N_EDGES), dma(N_EDGES), dma(8), dma(8),
        ],
        compiler_params=remote_params(0),
    )(
        hidden_in, norm_gain.reshape(TP, 1, ROWS), norm_bias.reshape(TP, 1, ROWS),
        qkv_weight, qkv_bias.reshape(3, 1, ROWS),
    )

    shared, oa, ob = pl.pallas_call(
        share_kernel,
        name="share",
        out_shape=(
            jax.ShapeDtypeStruct((4, 3, ROWS, ROWS), BF16),
            jax.ShapeDtypeStruct((NY, NX, NZ, 16, ROWS), BF16),
            jax.ShapeDtypeStruct((NX, NY, NZ, 16, ROWS), BF16),
        ),
        in_specs=[VMEM_SPEC] * 2,
        out_specs=(VMEM_SPEC,) * 3,
        scratch_shapes=[dma(3), dma(2), dma(2), dma(N_EDGES), dma(N_EDGES), dma(3), dma(3)],
        compiler_params=remote_params(1),
    )(qkv, out_block)

    seq_index = lax.axis_index("seq")
    local = seq_index % 4
    length = lax.dynamic_index_in_dim(cached_len, seq_index // 4, 0, keepdims=False)
    numbers = jnp.stack([local * SLOTS - length, local]).astype(jnp.int32)
    bias = lax.dynamic_slice_in_dim(jnp.asarray(bias_table()), lax.axis_index("tp") * 2, 2, 0)

    part, lse = pl.pallas_call(
        attend_kernel,
        name="attend",
        grid=(4,),
        out_shape=(
            jax.ShapeDtypeStruct((4, ROWS, ROWS), BF16),
            jax.ShapeDtypeStruct((4, 8, ROWS), F32),
        ),
        in_specs=[
            SMEM_SPEC,
            pl.BlockSpec((1, 1, ROWS, ROWS), lambda j: (j, 0, 0, 0)),
            VMEM_SPEC, VMEM_SPEC, VMEM_SPEC, VMEM_SPEC,
        ],
        out_specs=(
            pl.BlockSpec((1, ROWS, ROWS), lambda j: (j, 0, 0)),
            pl.BlockSpec((1, 8, ROWS), lambda j: (j, 0, 0)),
        ),
        scratch_shapes=[
            pltpu.VMEM((2, SLOTS + ROWS, ROWS), BF16),
            pltpu.VMEM((2, SLOTS + ROWS, ROWS), BF16),
        ],
        compiler_params=pltpu.CompilerParams(vmem_limit_bytes=48 << 20),
    )(numbers, shared, key_cache, value_cache, qkv, bias)

    mixed = pl.pallas_call(
        output_kernel,
        name="output",
        out_shape=jax.ShapeDtypeStruct((ROWS, ROWS), BF16),
        in_specs=[VMEM_SPEC] * 5,
        out_specs=VMEM_SPEC,
        scratch_shapes=[
            pltpu.VMEM((4, ROWS, ROWS), BF16),
            pltpu.VMEM((4, 8, ROWS), F32),
            pltpu.VMEM((ROWS, ROWS), BF16),
            pltpu.VMEM((TP, ROWS, ROWS), BF16),
            dma(3), dma(6), dma(6), dma(8), dma(8),
        ],
        compiler_params=remote_params(2),
    )(part, lse, oa, ob, out_bias.reshape(1, ROWS))

    block = pl.BlockSpec((ROWS, ROWS), lambda j: (j, 0))
    keys_new, values_new = pl.pallas_call(
        cache_kernel,
        name="cache",
        grid=(SLOTS // ROWS,),
        out_shape=(jax.ShapeDtypeStruct((SLOTS, ROWS), BF16),) * 2,
        in_specs=[SMEM_SPEC, VMEM_SPEC, block, block],
        out_specs=(block, block),
        scratch_shapes=[pltpu.VMEM((4, SPAN + 2 * PAD, HEAD_DIM), F32)],
        compiler_params=pltpu.CompilerParams(vmem_limit_bytes=32 << 20),
    )(numbers, shared, key_cache, value_cache)
    return (mixed, keys_new, values_new)


def solution(mesh):
    placed = (
        P("seq", "tp"),
        P(),
        P(),
        P(None, "seq", "tp"),
        P(None, "tp"),
        P("tp", "seq"),
        P("tp"),
        P("seq", "tp"),
        P("seq", "tp"),
        P(),
    )
    return jax.shard_map(
        on_device,
        mesh=mesh,
        in_specs=placed,
        out_specs=(P("seq", "tp"), P("seq", "tp"), P("seq", "tp")),
        check_vma=False,
    )
```

```python
import functools
import math

import jax
import jax.numpy as jnp
import numpy as np
from jax import lax
from jax.experimental import pallas as pl
from jax.experimental.pallas import tpu as pltpu
from jax.sharding import PartitionSpec as P

HEADS = 16
HEAD_DIM = 128
REQS = 16
SPAN = 1024
NX, NY, NZ = 4, 8, 2
TP = 8
ROWS = 256
SLOTS = 2304
LOG2E = 1.4426950408889634
MESH = pl.DeviceIdType.MESH
BF16 = jnp.bfloat16
F32 = jnp.float32
VMEM_SPEC = pl.BlockSpec(memory_space=pltpu.VMEM)
SMEM_SPEC = pl.BlockSpec(memory_space=pltpu.SMEM)


class Node:
    def __init__(self, tree, ox, oy, way, parent):
        self.tree, self.ox, self.oy, self.way, self.parent = tree, ox, oy, way, parent
        self.depth = 0 if parent is None else parent.depth + 1
        self.kids = []
        self.sem = None
        if parent is not None:
            parent.kids.append(self)


def build_tree(tree):
    root = Node(tree, 0, 0, None, None)

    def ring(start, axis, far_up):
        size = (NX, NY)[axis]
        for sign in (1, -1):
            most = size // 2 - (0 if (sign == 1) == far_up else 1)
            node = start
            for _ in range(most):
                step = [0, 0]
                step[axis] = -sign
                node = Node(tree, node.ox + step[0], node.oy + step[1], (axis, sign), node)
                yield node

    first, second = (0, 1) if tree == 0 else (1, 0)
    nodes = [root] + list(ring(root, first, True))
    flip = {}
    for node in list(nodes):
        off = node.ox if first == 0 else node.oy
        nodes += list(ring(node, second, (off % 2 == 0) if first == 1 else off in (0, -1)))
    return nodes


TREES = [build_tree(0), build_tree(1)]
EDGES = []
for _tree in TREES:
    for _node in _tree:
        if _node.parent is not None:
            _node.sem = len(EDGES)
            EDGES.append(_node)
N_EDGES = len(EDGES)
ORDER = sorted(EDGES, key=lambda n: (n.depth, n.sem))


class Place:
    def __init__(self):
        self.s = lax.axis_index("seq")
        self.t = lax.axis_index("tp")
        self.x = lax.div(self.s, NY * NZ)
        self.y = lax.rem(lax.div(self.s, NZ), NY)
        self.z = lax.rem(self.s, NZ)
        self.zh = lax.div(self.t, 2)
        self.core = lax.rem(self.t, 2)

    def seq(self, x, y, z):
        return (x * NY + y) * NZ + z

    def beside(self, axis, sign):
        if axis == 0:
            return (self.seq(lax.rem(self.x + sign + NX, NX), self.y, self.z), self.t)
        return (self.seq(self.x, lax.rem(self.y + sign + NY, NY), self.z), self.t)

    def z_partner(self):
        return (self.seq(self.x, self.y, 1 - self.z), self.t)

    def y_partner(self):
        return (self.seq(self.x, self.y + 1 - 2 * lax.rem(self.y, 2), self.z), self.t)

    def diagonal(self):
        return (self.seq(self.x, self.y + 1 - 2 * lax.rem(self.y, 2), 1 - self.z), self.t)

    def core_partner(self):
        return (self.s, self.zh * 2 + 1 - self.core)

    def up(self, hops):
        return (self.s, lax.rem(self.zh + hops + 4, 4) * 2 + self.core)

    def piece(self, bufs, node):
        ax = lax.rem(self.x + node.ox + NX, NX)
        ay = lax.rem(self.y + node.oy + NY, NY)
        if node.tree == 0:
            return bufs[0].at[ay, ax]
        return bufs[1].at[ax, ay]


def remote(src, dst, send_sem, recv_sem, device):
    return pltpu.make_async_remote_copy(
        src_ref=src, dst_ref=dst, send_sem=send_sem, recv_sem=recv_sem,
        device_id=device, device_id_type=MESH,
    )


class Gather:
    def __init__(self, place, halves, bufs, local_sem, zsend, zrecv, send, recv):
        self.p, self.halves, self.bufs = place, halves, bufs
        self.local_sem, self.zsend, self.zrecv, self.send, self.recv = local_sem, zsend, zrecv, send, recv
        self.sent = []

    def own(self, k):
        p = self.p
        return self.bufs[0].at[p.y, p.x, p.z] if k == 0 else self.bufs[1].at[p.x, p.y, p.z]

    def other(self, k):
        p = self.p
        return self.bufs[0].at[p.y, p.x, 1 - p.z] if k == 0 else self.bufs[1].at[p.x, p.y, 1 - p.z]

    def begin(self):
        self.locals = []
        for k in (0, 1):
            src = self.own(k) if self.halves is None else self.halves[k]
            copy = remote(src, self.own(k), self.zsend.at[k], self.zrecv.at[k], self.p.z_partner())
            copy.start()
            self.sent.append(copy)
        if self.halves is None:
            return
        for k in (0, 1):
            copy = pltpu.make_async_copy(self.halves[k], self.own(k), self.local_sem.at[k])
            copy.start()
            self.locals.append(copy)

    def forward(self, node):
        for kid in node.kids:
            piece = self.p.piece(self.bufs, node)
            copy = remote(piece, piece, self.send.at[kid.sem], self.recv.at[kid.sem], self.p.beside(*kid.way))
            copy.start()
            self.sent.append(copy)

    def roots(self):
        for k in (0, 1):
            if self.locals:
                self.locals[k].wait()
            other = self.other(k)
            remote(other, other, self.zsend.at[k], self.zrecv.at[k], self.p.z_partner()).wait_recv()
            self.forward(TREES[k][0])

    def take(self, node):
        piece = self.p.piece(self.bufs, node)
        way = (node.way[0], -node.way[1])
        remote(piece, piece, self.send.at[node.sem], self.recv.at[node.sem], self.p.beside(*way)).wait_recv()
        self.forward(node)

    def finish(self):
        for copy in self.sent:
            copy.wait_send()


class TpGather:
    def __init__(self, place, src, buf, local_sem, send, recv):
        self.p, self.src, self.buf = place, src, buf
        self.local_sem, self.send, self.recv = local_sem, send, recv
        self.sent = []

    def block(self, hops, mine=True):
        p = self.p
        core = p.core if mine else 1 - p.core
        return self.buf.at[lax.rem(p.zh + hops + 4, 4) * 2 + core]

    def copy(self, src, dst, index, device):
        return remote(src, dst, self.send.at[index], self.recv.at[index], device)

    def start(self, src, dst, index, device):
        copy = self.copy(src, dst, index, device)
        copy.start()
        self.sent.append(copy)

    def begin(self):
        p = self.p
        self.start(self.src, self.block(0), 0, p.up(1))
        self.start(self.src, self.block(0), 1, p.up(-1))
        self.start(self.src, self.block(0), 4, p.core_partner())
        self.local = pltpu.make_async_copy(self.src, self.block(0), self.local_sem)
        self.local.start()

    def near(self):
        p = self.p
        half = ROWS // 2
        low, high = self.block(-1), self.block(1)
        self.copy(low, low, 0, p.up(-1)).wait_recv()
        self.start(low.at[pl.ds(0, half)], low.at[pl.ds(0, half)], 2, p.up(1))
        self.start(low, low, 5, p.core_partner())
        self.copy(high, high, 1, p.up(1)).wait_recv()
        self.start(high.at[pl.ds(half, half)], high.at[pl.ds(half, half)], 3, p.up(-1))
        self.start(high, high, 6, p.core_partner())

    def far(self):
        p = self.p
        half = ROWS // 2
        block = self.block(2)
        lower, upper = block.at[pl.ds(0, half)], block.at[pl.ds(half, half)]
        self.copy(lower, lower, 2, p.up(-1)).wait_recv()
        self.copy(upper, upper, 3, p.up(1)).wait_recv()
        self.start(block, block, 7, p.core_partner())

    def rest(self):
        self.local.wait()
        for index, hops in ((4, 0), (5, -1), (6, 1), (7, 2)):
            block = self.block(hops, mine=False)
            self.copy(block, block, index, self.p.core_partner()).wait_recv()

    def finish(self):
        for copy in self.sent:
            copy.wait_send()


def weight_rows(a_ref, b_ref, seqs, pick):
    parts = []
    for s in seqs:
        x, y, z = s // (NY * NZ), (s // NZ) % NY, s % NZ
        parts.append(a_ref[(y, x, z) + pick])
        parts.append(b_ref[(x, y, z) + pick])
    return jnp.concatenate(parts, axis=0)


def layer_kernel(
    length_ref, hidden_hbm, gain_hbm, shift_hbm, weight_hbm, bias_hbm, out_weight_hbm, out_bias_hbm,
    keys_hbm, values_hbm, table_hbm,
    out_ref, fresh_all,
    hid, norm, qa, qb, ka, kb, oa, ob, gain, shift, bias, out_bias, table, keys, values,
    kaug, vaug, kfresh, vfresh, queries, acc, tops, parts, sides, part_out, side_out, mine, att,
    load_sem, local_sem, move_sem, zsend, zrecv, send, recv, hsend, hrecv, gsend, grecv, psend, precv, tsend, trecv,
):
    p = Place()
    peers = [None, p.z_partner(), p.y_partner(), p.diagonal()]
    local = lax.rem(p.s, 4)
    target_seq = lax.rem(p.s, 8) * 8 + p.t
    target = (target_seq, lax.div(p.s, 8))
    source = (p.t * 8 + lax.div(p.s, 8), lax.rem(p.s, 8))
    away = target_seq != p.s
    away = jnp.logical_or(away, target[1] != p.t)
    steady = peers[1:] + [p.core_partner(), p.up(1), p.up(-1),
                          p.beside(0, 1), p.beside(0, -1), p.beside(1, 1), p.beside(1, -1)]
    barrier = pltpu.get_barrier_semaphore()
    for device in steady:
        pl.semaphore_signal(barrier, inc=1, device_id=device, device_id_type=MESH)

    @pl.when(away)
    def _():
        for device in (target, source):
            pl.semaphore_signal(barrier, inc=1, device_id=device, device_id_type=MESH)

    loads = {}
    for index, (name, src, dst) in enumerate((
        ("gain", gain_hbm, gain), ("shift", shift_hbm, shift), ("bias", bias_hbm, bias),
        ("out_bias", out_bias_hbm, out_bias), ("table", table_hbm.at[pl.ds(p.t * 2, 2)], table),
        ("keys", keys_hbm, keys), ("values", values_hbm, values),
    )):
        loads[name] = pltpu.make_async_copy(src, dst, load_sem.at[index])
        loads[name].start()

    pl.semaphore_wait(barrier, len(steady) + 2 * away.astype(jnp.int32))

    def gather(index, halves, bufs):
        return Gather(p, halves, bufs, local_sem.at[index], zsend.at[index], zrecv.at[index],
                      send.at[index], recv.at[index])

    lower, upper = pl.ds(0, 16), pl.ds(16, 16)
    q_gather = gather(0, [weight_hbm.at[0, lower], weight_hbm.at[0, upper]], (qa, qb))
    kv_gather = gather(1, [weight_hbm.at[pl.ds(1, 2), lower], weight_hbm.at[pl.ds(1, 2), upper]], (ka, kb))
    o_gather = gather(2, None, (oa, ob))
    tokens = TpGather(p, hidden_hbm, hid, local_sem.at[2, 0], hsend, hrecv)
    q_gather.begin()
    tokens.begin()

    tx, ty, tz = lax.div(target_seq, 16), lax.rem(lax.div(target_seq, 2), NY), lax.rem(target_seq, 2)
    places = [oa.at[ty, tx, tz], ob.at[tx, ty, tz]]
    pieces = [out_weight_hbm.at[lower], out_weight_hbm.at[upper]]
    moved = [remote(pieces[k], places[k], move_sem.at[k], move_sem.at[2 + k], target) for k in (0, 1)]
    stay = [pltpu.make_async_copy(pieces[k], places[k], move_sem.at[4 + k]) for k in (0, 1)]

    @pl.when(away)
    def _():
        for copy in moved:
            copy.start()

    @pl.when(jnp.logical_not(away))
    def _():
        for copy in stay:
            copy.start()

    kv_gather.begin()
    q_gather.roots()

    length = length_ref[lax.div(p.s, 4)]
    first = local * SLOTS - length

    def aux(count, start, cached):
        place = lax.broadcasted_iota(jnp.int32, (count, HEAD_DIM), 0) + start
        lane = lax.broadcasted_iota(jnp.int32, (count, HEAD_DIM), 1)
        high = lax.shift_right_arithmetic(place, 7)
        low = place - high * 128
        number = jnp.where(lane < 3, high, jnp.where(lane < 6, low, 0)).astype(F32)
        if cached:
            number = jnp.where(place >= 0, jnp.where(lane == 6, -1e30, 0.0), number)
        return number.astype(BF16)

    def ones(count):
        return jnp.where(lax.broadcasted_iota(jnp.int32, (count, HEAD_DIM), 1) == 0, 1.0, 0.0).astype(BF16)

    columns = [slice(0, HEAD_DIM), slice(HEAD_DIM, 2 * HEAD_DIM)]

    def prepare_keys():
        loads["keys"].wait()
        number = aux(SLOTS, first, True)
        alive = lax.broadcasted_iota(jnp.int32, (SLOTS, HEAD_DIM), 0) + first < 0
        for head in range(2):
            kaug[head, :, :HEAD_DIM] = jnp.where(alive, keys[:, columns[head]].astype(F32), 0.0).astype(BF16)
            kaug[head, :, HEAD_DIM:] = number

    def prepare_values():
        loads["values"].wait()
        for head in range(2):
            vaug[head, :, :HEAD_DIM] = values[:, columns[head]]
            vaug[head, :, HEAD_DIM:] = ones(SLOTS)

    def normalise(start, rows):
        numbers = [hid[t, start:start + rows, :].astype(F32) for t in range(TP)]
        mean = jnp.sum(functools.reduce(jnp.add, numbers), axis=1, keepdims=True) * (1.0 / (TP * ROWS))
        numbers = [v - mean for v in numbers]
        squares = functools.reduce(jnp.add, [v * v for v in numbers])
        variance = jnp.sum(squares, axis=1, keepdims=True) * (1.0 / (TP * ROWS))
        scale = lax.rsqrt(variance + 1e-05)
        for t in range(TP):
            cols = slice(t * ROWS, (t + 1) * ROWS)
            norm[t, start:start + rows, :] = (numbers[t] * scale * gain[:, cols] + shift[:, cols]).astype(BF16)

    def project(bufs, pick, row):
        total = None
        for t in range(TP):
            rows = weight_rows(bufs[0], bufs[1], range(t * 8, t * 8 + 8), pick)
            part = jnp.dot(norm[t], rows, preferred_element_type=F32)
            total = part if total is None else total + part
        return total + bias[row:row + 1, :]

    levels = [[n for n in ORDER if n.depth == d] for d in range(7)]

    def step(who, depth):
        for node in levels[depth]:
            who.take(node)

    prepare_keys()
    step(q_gather, 1)
    tokens.near()
    step(q_gather, 2)
    prepare_values()
    tokens.far()
    step(q_gather, 3)
    tokens.rest()
    kv_gather.roots()
    for name in ("gain", "shift", "bias", "out_bias", "table"):
        loads[name].wait()
    step(q_gather, 4)
    normalise(0, 128)
    step(q_gather, 5)
    normalise(128, 128)
    step(q_gather, 6)
    step(kv_gather, 1)
    queries[local] = (project((qa, qb), (), 0) * (LOG2E / math.sqrt(HEAD_DIM))).astype(BF16)
    sent = []

    def exchange(src, dst, sems, index, peer):
        copy = remote(src, dst, sems[0].at[index], sems[1].at[index], peer)
        copy.start()
        sent.append(copy)

    def arrived(dst, sems, index, peer):
        remote(dst, dst, sems[0].at[index], sems[1].at[index], peer).wait_recv()

    step(kv_gather, 2)
    for k in (1, 2, 3):
        exchange(queries.at[local], queries.at[local], (gsend, grecv), k, peers[k])

    def query_of(block, head):
        side = jnp.broadcast_to(table[head], (ROWS, HEAD_DIM)).astype(BF16)
        return jnp.concatenate([queries[block, :, columns[head]], side], axis=1)

    nt = (((1,), (1,)), ((), ()))

    def attend(k, block):
        for head in range(2):
            score = lax.dot_general(query_of(block, head), kaug[head], nt, preferred_element_type=F32)
            top = jnp.max(score, axis=1, keepdims=True)
            weight = jnp.exp2(score - top).astype(BF16)
            acc[2 * k + head] = jnp.dot(weight, vaug[head], preferred_element_type=F32)
            tops[2 * k + head] = jnp.broadcast_to(top, (ROWS, HEAD_DIM))

    blocks = [local] + [lax.rem(peer[0], 4) for peer in peers[1:]]
    attend(0, blocks[0])
    step(kv_gather, 3)
    arrived(queries.at[blocks[1]], (gsend, grecv), 1, peers[1])
    attend(1, blocks[1])
    step(kv_gather, 4)

    @pl.when(away)
    def _():
        for k in (0, 1):
            own = o_gather.own(k)
            remote(own, own, move_sem.at[k], move_sem.at[2 + k], source).wait_recv()
            moved[k].wait_send()

    @pl.when(jnp.logical_not(away))
    def _():
        for copy in stay:
            copy.wait()

    o_gather.begin()
    arrived(queries.at[blocks[2]], (gsend, grecv), 2, peers[2])
    attend(2, blocks[2])
    step(kv_gather, 5)
    arrived(queries.at[blocks[3]], (gsend, grecv), 3, peers[3])
    attend(3, blocks[3])
    step(kv_gather, 6)
    o_gather.roots()

    for which in range(2):
        fresh_all[local, which] = project((ka, kb), (which,), 1 + which).astype(BF16)
    number = aux(ROWS, local * ROWS, False)
    for head in range(2):
        kfresh[head, :, :HEAD_DIM] = fresh_all[local, 0, :, columns[head]]
        kfresh[head, :, HEAD_DIM:] = number
        vfresh[head, :, :HEAD_DIM] = fresh_all[local, 1, :, columns[head]]
        vfresh[head, :, HEAD_DIM:] = ones(ROWS)
    step(o_gather, 1)

    def attend_fresh(k, block, put_part, put_side):
        row = lax.broadcasted_iota(jnp.int32, (ROWS, ROWS), 0) + block * ROWS
        column = lax.broadcasted_iota(jnp.int32, (ROWS, ROWS), 1) + local * ROWS
        lses = []
        for head in range(2):
            score = lax.dot_general(query_of(block, head), kfresh[head], nt, preferred_element_type=F32)
            score = jnp.where(column <= row, score, -1e30)
            before = tops[2 * k + head][:, :1]
            top = jnp.maximum(before, jnp.max(score, axis=1, keepdims=True))
            weight = jnp.exp2(score - top).astype(BF16)
            both = jnp.dot(weight, vfresh[head], preferred_element_type=F32)
            both += acc[2 * k + head] * jnp.exp2(before - top)
            total = both[:, HEAD_DIM:HEAD_DIM + 1]
            put_part(columns[head], (both[:, :HEAD_DIM] / total).astype(BF16))
            lses.append(top + jnp.log2(total))
        lane = lax.broadcasted_iota(jnp.int32, (ROWS, HEAD_DIM), 1)
        put_side(jnp.transpose(jnp.where(lane == 0, lses[0], lses[1]))[:8])

    def put(ref, index):
        def store(cols, value):
            ref[index, :, cols] = value
        return store

    def put_all(ref, index):
        def store(value):
            ref[index] = value
        return store

    def send_part(k):
        exchange(part_out.at[k], parts.at[local], (psend, precv), k, peers[k])
        exchange(side_out.at[k], sides.at[local], (psend, precv), 4 + k, peers[k])

    attend_fresh(3, blocks[3], put(part_out, 3), put_all(side_out, 3))
    attend_fresh(2, blocks[2], put(part_out, 2), put_all(side_out, 2))
    send_part(3)
    attend_fresh(1, blocks[1], put(part_out, 1), put_all(side_out, 1))
    send_part(2)
    attend_fresh(0, blocks[0], put(parts, local), put_all(sides, local))
    send_part(1)
    exchange(fresh_all.at[local], fresh_all.at[local], (gsend, grecv), 4, peers[1])
    exchange(fresh_all.at[local], fresh_all.at[local], (gsend, grecv), 5, peers[2])
    step(o_gather, 2)
    for k in (3, 2, 1):
        arrived(parts.at[blocks[k]], (psend, precv), k, peers[k])
        arrived(sides.at[blocks[k]], (psend, precv), 4 + k, peers[k])
    stats = [sides[k] for k in range(4)]
    top = functools.reduce(jnp.maximum, stats)
    shares = [jnp.exp2(stat - top) for stat in stats]
    total = functools.reduce(jnp.add, shares)
    shares = [jnp.transpose(jnp.concatenate([share / total] * 16, axis=0)) for share in shares]
    for head in range(2):
        terms = [parts[k, :, columns[head]].astype(F32) * shares[k][:, head:head + 1] for k in range(4)]
        mine[:, columns[head]] = functools.reduce(jnp.add, terms).astype(BF16)
    tokens.finish()
    finals = TpGather(p, mine, att, local_sem.at[2, 1], tsend, trecv)
    finals.begin()
    step(o_gather, 3)
    finals.near()
    step(o_gather, 4)
    arrived(fresh_all.at[blocks[1]], (gsend, grecv), 4, peers[1])
    exchange(fresh_all.at[blocks[1]], fresh_all.at[blocks[1]], (gsend, grecv), 6, peers[2])
    finals.far()
    step(o_gather, 5)
    step(o_gather, 6)
    finals.rest()
    result = None
    for t in range(TP):
        rows = weight_rows(oa, ob, range(t, 64, TP), ())
        term = lax.dot_general(att[t], rows, nt, preferred_element_type=F32)
        result = term if result is None else result + term
    out_ref[...] = (result + out_bias[...]).astype(BF16)
    arrived(fresh_all.at[blocks[2]], (gsend, grecv), 5, peers[2])
    arrived(fresh_all.at[blocks[3]], (gsend, grecv), 6, peers[2])
    for copy in sent:
        copy.wait_send()
    for who in (q_gather, kv_gather, o_gather, finals):
        who.finish()


PAD = ROWS + 32


def cache_kernel(numbers_ref, all_ref, keys_ref, values_ref, keys_out, values_out, fresh):
    step = pl.program_id(0)

    @pl.when(step == 0)
    def _():
        for k in range(2):
            for h in range(2):
                fresh[2 * k + h, :PAD] = jnp.zeros((PAD, HEAD_DIM), F32)
                fresh[2 * k + h, PAD + SPAN:] = jnp.zeros((PAD, HEAD_DIM), F32)
                for block in range(4):
                    rows = all_ref[block, k, :, h * HEAD_DIM:(h + 1) * HEAD_DIM]
                    fresh[2 * k + h, PAD + block * ROWS:PAD + (block + 1) * ROWS] = rows.astype(F32)

    start = step * ROWS + numbers_ref[0]
    touched = (start > -ROWS) & (start < SPAN)

    @pl.when(touched)
    def _():
        begin = jnp.clip(start, -ROWS, SPAN)
        place = lax.broadcasted_iota(jnp.int32, (ROWS, HEAD_DIM), 0) + begin
        inside = (place >= 0) & (place < SPAN)
        for k, (old, new) in enumerate(((keys_ref, keys_out), (values_ref, values_out))):
            for h in range(2):
                cols = slice(h * HEAD_DIM, (h + 1) * HEAD_DIM)
                rows = fresh[2 * k + h, pl.ds(begin + PAD, ROWS), :]
                new[:, cols] = jnp.where(inside, rows, old[:, cols].astype(F32)).astype(BF16)

    @pl.when(jnp.logical_not(touched))
    def _():
        keys_out[...] = keys_ref[...]
        values_out[...] = values_ref[...]


def round_bf16(value):
    return np.asarray(np.asarray(value, np.float32).astype(jnp.bfloat16), np.float64)


def bias_table():
    table = np.zeros((HEADS, 1, HEAD_DIM), np.float64)
    for head in range(HEADS):
        slope = 2.0 ** (-8.0 * (head + 1) / HEADS) * LOG2E
        for column, value in ((0, slope * 128.0), (3, slope)):
            rest = value
            for k in range(3):
                table[head, 0, column + k] = round_bf16(rest)
                rest = rest - table[head, 0, column + k]
        table[head, 0, 6] = 1.0
    return table.astype(np.float32)


def dma(*count):
    return pltpu.SemaphoreType.DMA(count)


def on_device(
    hidden_in, norm_gain, norm_bias, qkv_weight, qkv_bias, out_weight, out_bias, key_cache, value_cache, cached_len,
):
    any_spec = pl.BlockSpec(memory_space=pl.ANY)

    def vm(*shape, dtype=BF16):
        return pltpu.VMEM(shape, dtype)

    mixed, shared = pl.pallas_call(
        layer_kernel,
        name="layer",
        out_shape=(
            jax.ShapeDtypeStruct((ROWS, ROWS), BF16),
            jax.ShapeDtypeStruct((4, 2, ROWS, ROWS), BF16),
        ),
        in_specs=[SMEM_SPEC] + [any_spec] * 10,
        out_specs=(VMEM_SPEC, VMEM_SPEC),
        scratch_shapes=[
            vm(TP, ROWS, ROWS), vm(TP, ROWS, ROWS),
            vm(NY, NX, NZ, 16, ROWS), vm(NX, NY, NZ, 16, ROWS),
            vm(NY, NX, NZ, 2, 16, ROWS), vm(NX, NY, NZ, 2, 16, ROWS),
            vm(NY, NX, NZ, 16, ROWS), vm(NX, NY, NZ, 16, ROWS),
            vm(1, TP * ROWS, dtype=F32), vm(1, TP * ROWS, dtype=F32), vm(3, ROWS, dtype=F32), vm(1, ROWS, dtype=F32),
            vm(2, 1, HEAD_DIM, dtype=F32), vm(SLOTS, ROWS), vm(SLOTS, ROWS),
            vm(2, SLOTS, ROWS), vm(2, SLOTS, ROWS), vm(2, ROWS, ROWS), vm(2, ROWS, ROWS),
            vm(4, ROWS, ROWS), vm(8, ROWS, ROWS, dtype=F32), vm(8, ROWS, HEAD_DIM, dtype=F32),
            vm(4, ROWS, ROWS), vm(4, 8, ROWS, dtype=F32), vm(4, ROWS, ROWS), vm(4, 8, ROWS, dtype=F32),
            vm(ROWS, ROWS), vm(TP, ROWS, ROWS),
            dma(7), dma(3, 2), dma(6), dma(3, 2), dma(3, 2), dma(3, N_EDGES), dma(3, N_EDGES),
            dma(8), dma(8), dma(7), dma(7), dma(8), dma(8), dma(8), dma(8),
        ],
        compiler_params=pltpu.CompilerParams(collective_id=0, has_side_effects=True, vmem_limit_bytes=56 << 20),
    )(
        cached_len, hidden_in, norm_gain.reshape(1, TP * ROWS), norm_bias.reshape(1, TP * ROWS),
        qkv_weight, qkv_bias, out_weight.T, out_bias.reshape(1, ROWS), key_cache, value_cache,
        jnp.asarray(bias_table()),
    )

    seq_index = lax.axis_index("seq")
    length = lax.dynamic_index_in_dim(cached_len, seq_index // 4, 0, keepdims=False)
    numbers = (seq_index % 4 * SLOTS - length).astype(jnp.int32).reshape(1)

    block = pl.BlockSpec((ROWS, ROWS), lambda j: (j, 0))
    keys_new, values_new = pl.pallas_call(
        cache_kernel,
        name="cache",
        grid=(SLOTS // ROWS,),
        out_shape=(jax.ShapeDtypeStruct((SLOTS, ROWS), BF16),) * 2,
        in_specs=[SMEM_SPEC, VMEM_SPEC, block, block],
        out_specs=(block, block),
        scratch_shapes=[pltpu.VMEM((4, SPAN + 2 * PAD, HEAD_DIM), F32)],
        compiler_params=pltpu.CompilerParams(vmem_limit_bytes=32 << 20),
    )(numbers, shared, key_cache, value_cache)
    return (mixed, keys_new, values_new)


def solution(mesh):
    placed = (
        P("seq", "tp"),
        P(),
        P(),
        P(None, "seq", "tp"),
        P(None, "tp"),
        P("tp", "seq"),
        P("tp"),
        P("seq", "tp"),
        P("seq", "tp"),
        P(),
    )
    return jax.shard_map(
        on_device,
        mesh=mesh,
        in_specs=placed,
        out_specs=(P("seq", "tp"), P("seq", "tp"), P("seq", "tp")),
        check_vma=False,
    )
```

```python
import functools
import math

import jax
import jax.numpy as jnp
import numpy as np
from jax import lax
from jax.experimental import pallas as pl
from jax.experimental.pallas import tpu as pltpu
from jax.sharding import PartitionSpec as P

HEADS = 16
HEAD_DIM = 128
REQS = 16
SPAN = 1024
NX, NY, NZ = 4, 8, 2
TP = 8
ROWS = 256
PAD = ROWS + 32
SLOTS = 2304
LOG2E = 1.4426950408889634
MESH = pl.DeviceIdType.MESH
BF16 = jnp.bfloat16
F32 = jnp.float32
VMEM_SPEC = pl.BlockSpec(memory_space=pltpu.VMEM)
SMEM_SPEC = pl.BlockSpec(memory_space=pltpu.SMEM)


class Node:
    def __init__(self, tree, ox, oy, way, parent):
        self.tree, self.ox, self.oy, self.way, self.parent = tree, ox, oy, way, parent
        self.depth = 0 if parent is None else parent.depth + 1
        self.kids = []
        self.sem = None
        if parent is not None:
            parent.kids.append(self)

    def grow(self, axis, hops):
        return Node(self.tree, self.ox - hops * (axis == 0), self.oy - hops * (axis == 1), (axis, hops), self)


def deep_ring(start, axis, far_up):
    size = (NX, NY)[axis]
    nodes = []
    for sign in (1, -1):
        node = start
        for _ in range(size // 2 - (0 if (sign == 1) == far_up else 1)):
            node = node.grow(axis, sign)
            nodes.append(node)
    return nodes


def shallow_ring(start, axis, far_up):
    if axis == 0:
        return [start.grow(0, 1), start.grow(0, -1), start.grow(0, 2 if far_up else -2)]
    near = [start.grow(1, 1), start.grow(1, -1)]
    far = [start.grow(1, 3), start.grow(1, -3)]
    more = [near[0].grow(1, 1), near[1].grow(1, -1), far[0].grow(1, 1) if far_up else far[1].grow(1, -1)]
    return near + far + more


class Forest:
    def __init__(self, ring):
        self.roots, self.edges = [], []
        for tree in (0, 1):
            root = Node(tree, 0, 0, None, None)
            nodes = [root] + ring(root, tree, True)
            for node in list(nodes):
                off = node.oy if tree else node.ox
                nodes += ring(node, 1 - tree, off % 2 == 0 if tree else off in (0, -1))
            self.roots.append(root)
            self.edges += nodes[1:]
        for index, node in enumerate(self.edges):
            node.sem = index
        self.depth = max(node.depth for node in self.edges)
        order = sorted(self.edges, key=lambda n: (abs(n.way[1]), n.sem))
        self.levels = [[n for n in order if n.depth == d] for d in range(self.depth + 1)]


DEEP, SHALLOW = Forest(deep_ring), Forest(shallow_ring)
N_EDGES = len(DEEP.edges)


class Place:
    def __init__(self):
        self.s = lax.axis_index("seq")
        self.t = lax.axis_index("tp")
        self.x = lax.div(self.s, NY * NZ)
        self.y = lax.rem(lax.div(self.s, NZ), NY)
        self.z = lax.rem(self.s, NZ)
        self.zh = lax.div(self.t, 2)
        self.core = lax.rem(self.t, 2)

    def seq(self, x, y, z):
        return (x * NY + y) * NZ + z

    def beside(self, axis, sign):
        if axis == 0:
            return (self.seq(lax.rem(self.x + sign + NX, NX), self.y, self.z), self.t)
        return (self.seq(self.x, lax.rem(self.y + sign + NY, NY), self.z), self.t)

    def z_partner(self):
        return (self.seq(self.x, self.y, 1 - self.z), self.t)

    def y_partner(self):
        return (self.seq(self.x, self.y + 1 - 2 * lax.rem(self.y, 2), self.z), self.t)

    def diagonal(self):
        return (self.seq(self.x, self.y + 1 - 2 * lax.rem(self.y, 2), 1 - self.z), self.t)

    def core_partner(self):
        return (self.s, self.zh * 2 + 1 - self.core)

    def up(self, hops):
        return (self.s, lax.rem(self.zh + hops + 4, 4) * 2 + self.core)

    def piece(self, bufs, node):
        ax = lax.rem(self.x + node.ox + NX, NX)
        ay = lax.rem(self.y + node.oy + NY, NY)
        if node.tree == 0:
            return bufs[0].at[ay, ax]
        return bufs[1].at[ax, ay]


def remote(src, dst, send_sem, recv_sem, device):
    return pltpu.make_async_remote_copy(
        src_ref=src, dst_ref=dst, send_sem=send_sem, recv_sem=recv_sem,
        device_id=device, device_id_type=MESH,
    )


class Gather:
    def __init__(self, place, forest, halves, bufs, local_sem, zsend, zrecv, send, recv):
        self.p, self.forest, self.halves, self.bufs = place, forest, halves, bufs
        self.local_sem, self.zsend, self.zrecv, self.send, self.recv = local_sem, zsend, zrecv, send, recv
        self.sent = []

    def own(self, k):
        p = self.p
        return self.bufs[0].at[p.y, p.x, p.z] if k == 0 else self.bufs[1].at[p.x, p.y, p.z]

    def other(self, k):
        p = self.p
        return self.bufs[0].at[p.y, p.x, 1 - p.z] if k == 0 else self.bufs[1].at[p.x, p.y, 1 - p.z]

    def begin(self):
        self.locals = []
        for k in (0, 1):
            src = self.own(k) if self.halves is None else self.halves[k]
            copy = remote(src, self.own(k), self.zsend.at[k], self.zrecv.at[k], self.p.z_partner())
            copy.start()
            self.sent.append(copy)
        if self.halves is None:
            return
        for k in (0, 1):
            copy = pltpu.make_async_copy(self.halves[k], self.own(k), self.local_sem.at[k])
            copy.start()
            self.locals.append(copy)

    def forward(self, node):
        for kid in node.kids:
            piece = self.p.piece(self.bufs, node)
            copy = remote(piece, piece, self.send.at[kid.sem], self.recv.at[kid.sem], self.p.beside(*kid.way))
            copy.start()
            self.sent.append(copy)

    def roots(self):
        for k in (0, 1):
            if self.locals:
                self.locals[k].wait()
            other = self.other(k)
            remote(other, other, self.zsend.at[k], self.zrecv.at[k], self.p.z_partner()).wait_recv()
            self.forward(self.forest.roots[k])

    def take(self, node):
        piece = self.p.piece(self.bufs, node)
        way = (node.way[0], -node.way[1])
        remote(piece, piece, self.send.at[node.sem], self.recv.at[node.sem], self.p.beside(*way)).wait_recv()
        self.forward(node)

    def step(self, depth):
        for node in self.forest.levels[depth]:
            self.take(node)

    def finish(self):
        for copy in self.sent:
            copy.wait_send()


class TpGather:
    def __init__(self, place, src, buf, local_sem, send, recv):
        self.p, self.src, self.buf = place, src, buf
        self.local_sem, self.send, self.recv = local_sem, send, recv
        self.sent = []

    def block(self, hops, mine=True):
        p = self.p
        core = p.core if mine else 1 - p.core
        return self.buf.at[lax.rem(p.zh + hops + 4, 4) * 2 + core]

    def copy(self, src, dst, index, device):
        return remote(src, dst, self.send.at[index], self.recv.at[index], device)

    def start(self, src, dst, index, device):
        copy = self.copy(src, dst, index, device)
        copy.start()
        self.sent.append(copy)

    def begin(self):
        p = self.p
        self.start(self.src, self.block(0), 0, p.up(1))
        self.start(self.src, self.block(0), 1, p.up(-1))
        self.start(self.src, self.block(0), 4, p.core_partner())
        self.local = pltpu.make_async_copy(self.src, self.block(0), self.local_sem)
        self.local.start()

    def near(self):
        p = self.p
        half = ROWS // 2
        low, high = self.block(-1), self.block(1)
        self.copy(low, low, 0, p.up(-1)).wait_recv()
        self.start(low.at[pl.ds(0, half)], low.at[pl.ds(0, half)], 2, p.up(1))
        self.start(low, low, 5, p.core_partner())
        self.copy(high, high, 1, p.up(1)).wait_recv()
        self.start(high.at[pl.ds(half, half)], high.at[pl.ds(half, half)], 3, p.up(-1))
        self.start(high, high, 6, p.core_partner())

    def far(self):
        p = self.p
        half = ROWS // 2
        block = self.block(2)
        lower, upper = block.at[pl.ds(0, half)], block.at[pl.ds(half, half)]
        self.copy(lower, lower, 2, p.up(-1)).wait_recv()
        self.copy(upper, upper, 3, p.up(1)).wait_recv()
        self.start(block, block, 7, p.core_partner())

    def rest(self):
        self.local.wait()
        for index, hops in ((4, 0), (5, -1), (6, 1), (7, 2)):
            block = self.block(hops, mine=False)
            self.copy(block, block, index, self.p.core_partner()).wait_recv()

    def finish(self):
        for copy in self.sent:
            copy.wait_send()


def weight_rows(a_ref, b_ref, seqs, pick):
    parts = []
    for s in seqs:
        x, y, z = s // (NY * NZ), (s // NZ) % NY, s % NZ
        parts.append(a_ref[(y, x, z) + pick])
        parts.append(b_ref[(x, y, z) + pick])
    return jnp.concatenate(parts, axis=0)


def layer_kernel(
    length_ref, hidden_hbm, gain_hbm, shift_hbm, weight_hbm, bias_hbm, out_weight_hbm, out_bias_hbm,
    keys_hbm, values_hbm, table_hbm,
    out_ref, keys_out, values_out,
    fresh_all, fresh, hid, norm, qa, qb, ra, rb, gain, shift, bias, out_bias, table, keys, values,
    kaug, vaug, kfresh, vfresh, queries, acc, tops, parts, sides, part_out, side_out, mine, att,
    load_sem, local_sem, move_sem, zsend, zrecv, send, recv, hsend, hrecv, gsend, grecv, psend, precv, tsend, trecv,
):
    p = Place()
    peers = [None, p.z_partner(), p.y_partner(), p.diagonal()]
    local = lax.rem(p.s, 4)
    target_seq = lax.rem(p.s, 8) * 8 + p.t
    target = (target_seq, lax.div(p.s, 8))
    source = (p.t * 8 + lax.div(p.s, 8), lax.rem(p.s, 8))
    away = target_seq != p.s
    away = jnp.logical_or(away, target[1] != p.t)
    steady = peers[1:] + [p.core_partner(), p.up(1), p.up(-1),
                          p.beside(0, 1), p.beside(0, -1), p.beside(0, 2),
                          p.beside(1, 1), p.beside(1, -1), p.beside(1, 3), p.beside(1, -3)]
    barrier = pltpu.get_barrier_semaphore()
    for device in steady:
        pl.semaphore_signal(barrier, inc=1, device_id=device, device_id_type=MESH)

    @pl.when(away)
    def _():
        for device in (target, source):
            pl.semaphore_signal(barrier, inc=1, device_id=device, device_id_type=MESH)

    loads = {}
    for index, (name, src, dst) in enumerate((
        ("gain", gain_hbm, gain), ("shift", shift_hbm, shift), ("bias", bias_hbm, bias),
        ("out_bias", out_bias_hbm, out_bias), ("table", table_hbm.at[pl.ds(p.t * 2, 2)], table),
        ("keys", keys_hbm, keys), ("values", values_hbm, values),
    )):
        loads[name] = pltpu.make_async_copy(src, dst, load_sem.at[index])
        loads[name].start()

    pl.semaphore_wait(barrier, len(steady) + 2 * away.astype(jnp.int32))

    def gather(index, forest, halves, bufs):
        return Gather(p, forest, halves, bufs, local_sem.at[index], zsend.at[index], zrecv.at[index],
                      send.at[index], recv.at[index])

    lower, upper = pl.ds(0, 16), pl.ds(16, 16)
    q_gather = gather(0, SHALLOW, [weight_hbm.at[0, lower], weight_hbm.at[0, upper]], (qa, qb))
    rest = gather(1, DEEP, None, (ra, rb))
    tokens = TpGather(p, hidden_hbm, hid, local_sem.at[2, 0], hsend, hrecv)
    q_gather.begin()
    tokens.begin()

    tx, ty, tz = lax.div(target_seq, 16), lax.rem(lax.div(target_seq, 2), NY), lax.rem(target_seq, 2)
    pieces = [out_weight_hbm.at[lower], out_weight_hbm.at[upper]]
    places = [rb.at[tx, ty, tz, 2 + k] for k in (0, 1)]
    moved = [remote(pieces[k], places[k], move_sem.at[k], move_sem.at[2 + k], target) for k in (0, 1)]
    stay = [pltpu.make_async_copy(pieces[k], places[k], move_sem.at[4 + k]) for k in (0, 1)]

    @pl.when(away)
    def _():
        for copy in moved:
            copy.start()

    @pl.when(jnp.logical_not(away))
    def _():
        for copy in stay:
            copy.start()

    placed = [
        pltpu.make_async_copy(weight_hbm.at[pl.ds(1, 2), rows], own.at[pl.ds(0, 2)], local_sem.at[1, k])
        for k, (rows, own) in enumerate(((lower, rest.own(0)), (upper, rest.own(1))))
    ]
    for copy in placed:
        copy.start()
    q_gather.roots()

    length = length_ref[lax.div(p.s, 4)]
    first = local * SLOTS - length

    def aux(count, start, cached):
        place = lax.broadcasted_iota(jnp.int32, (count, HEAD_DIM), 0) + start
        lane = lax.broadcasted_iota(jnp.int32, (count, HEAD_DIM), 1)
        high = lax.shift_right_arithmetic(place, 7)
        low = place - high * 128
        number = jnp.where(lane < 3, high, jnp.where(lane < 6, low, 0)).astype(F32)
        if cached:
            number = jnp.where(place >= 0, jnp.where(lane == 6, -1e30, 0.0), number)
        return number.astype(BF16)

    def ones(count):
        return jnp.ones((count, HEAD_DIM), BF16)

    columns = [slice(0, HEAD_DIM), slice(HEAD_DIM, 2 * HEAD_DIM)]

    def prepare_keys():
        loads["keys"].wait()
        number = aux(SLOTS, first, True)
        alive = lax.broadcasted_iota(jnp.int32, (SLOTS, HEAD_DIM), 0) + first < 0
        for head in range(2):
            kaug[head, :, :HEAD_DIM] = jnp.where(alive, keys[:, columns[head]].astype(F32), 0.0).astype(BF16)
            kaug[head, :, HEAD_DIM:] = number

    def prepare_values():
        loads["values"].wait()
        for head in range(2):
            vaug[head, :, :HEAD_DIM] = values[:, columns[head]]
            vaug[head, :, HEAD_DIM:] = ones(SLOTS)

    def normalise(start, rows):
        numbers = [hid[t, start:start + rows, :].astype(F32) for t in range(TP)]
        mean = jnp.sum(functools.reduce(jnp.add, numbers), axis=1, keepdims=True) * (1.0 / (TP * ROWS))
        numbers = [v - mean for v in numbers]
        squares = functools.reduce(jnp.add, [v * v for v in numbers])
        variance = jnp.sum(squares, axis=1, keepdims=True) * (1.0 / (TP * ROWS))
        scale = lax.rsqrt(variance + 1e-05)
        for t in range(TP):
            cols = slice(t * ROWS, (t + 1) * ROWS)
            norm[t, start:start + rows, :] = (numbers[t] * scale * gain[:, cols] + shift[:, cols]).astype(BF16)

    def project(bufs, pick, row):
        total = None
        for t in range(TP):
            rows = weight_rows(bufs[0], bufs[1], range(t * 8, t * 8 + 8), pick)
            part = jnp.dot(norm[t], rows, preferred_element_type=F32)
            total = part if total is None else total + part
        return total + bias[row:row + 1, :]

    prepare_keys()
    q_gather.step(1)
    tokens.near()

    @pl.when(away)
    def _():
        for k in (0, 1):
            own = rb.at[p.x, p.y, p.z, 2 + k]
            remote(own, own, move_sem.at[k], move_sem.at[2 + k], source).wait_recv()
            moved[k].wait_send()

    @pl.when(jnp.logical_not(away))
    def _():
        for copy in stay:
            copy.wait()

    for copy in placed:
        copy.wait()
    rest.begin()
    prepare_values()
    rest.roots()
    q_gather.step(2)
    tokens.far()
    rest.step(1)
    q_gather.step(3)
    for name in ("gain", "shift", "bias", "out_bias", "table"):
        loads[name].wait()
    tokens.rest()
    normalise(0, 128)
    normalise(128, 128)
    queries[local] = (project((qa, qb), (), 0) * (LOG2E / math.sqrt(HEAD_DIM))).astype(BF16)
    sent = []

    def exchange(src, dst, sems, index, peer):
        copy = remote(src, dst, sems[0].at[index], sems[1].at[index], peer)
        copy.start()
        sent.append(copy)

    def arrived(dst, sems, index, peer):
        remote(dst, dst, sems[0].at[index], sems[1].at[index], peer).wait_recv()

    for k in (1, 2, 3):
        exchange(queries.at[local], queries.at[local], (gsend, grecv), k, peers[k])

    def query_of(block, head):
        side = jnp.broadcast_to(table[head], (ROWS, HEAD_DIM)).astype(BF16)
        return jnp.concatenate([queries[block, :, columns[head]], side], axis=1)

    nt = (((1,), (1,)), ((), ()))

    def attend(k, block):
        for head in range(2):
            score = lax.dot_general(query_of(block, head), kaug[head], nt, preferred_element_type=F32)
            top = jnp.max(score, axis=1, keepdims=True)
            weight = jnp.exp2(score - top).astype(BF16)
            acc[2 * k + head] = jnp.dot(weight, vaug[head], preferred_element_type=F32)
            tops[2 * k + head] = jnp.broadcast_to(top, (ROWS, HEAD_DIM))

    blocks = [local] + [lax.rem(peer[0], 4) for peer in peers[1:]]
    attend(0, blocks[0])
    rest.step(2)
    arrived(queries.at[blocks[1]], (gsend, grecv), 1, peers[1])
    attend(1, blocks[1])
    rest.step(3)
    arrived(queries.at[blocks[2]], (gsend, grecv), 2, peers[2])
    attend(2, blocks[2])
    rest.step(4)
    arrived(queries.at[blocks[3]], (gsend, grecv), 3, peers[3])
    attend(3, blocks[3])
    rest.step(5)
    rest.step(6)

    for which in range(2):
        fresh_all[local, which] = project((ra, rb), (which,), 1 + which).astype(BF16)
    exchange(fresh_all.at[local], fresh_all.at[local], (gsend, grecv), 4, peers[1])
    number = aux(ROWS, local * ROWS, False)
    for head in range(2):
        kfresh[head, :, :HEAD_DIM] = fresh_all[local, 0, :, columns[head]]
        kfresh[head, :, HEAD_DIM:] = number
        vfresh[head, :, :HEAD_DIM] = fresh_all[local, 1, :, columns[head]]
        vfresh[head, :, HEAD_DIM:] = ones(ROWS)

    def attend_fresh(k, block, put_part, put_side):
        row = lax.broadcasted_iota(jnp.int32, (ROWS, ROWS), 0) + block * ROWS
        column = lax.broadcasted_iota(jnp.int32, (ROWS, ROWS), 1) + local * ROWS
        lses = []
        for head in range(2):
            score = lax.dot_general(query_of(block, head), kfresh[head], nt, preferred_element_type=F32)
            score = jnp.where(column <= row, score, -1e30)
            before = tops[2 * k + head]
            top = jnp.maximum(before, jnp.max(score, axis=1, keepdims=True))
            weight = jnp.exp2(score - jnp.concatenate([top, top], axis=1)).astype(BF16)
            keep = jnp.exp2(before - top)
            both = jnp.dot(weight, vfresh[head], preferred_element_type=F32)
            number = both[:, :HEAD_DIM] + acc[2 * k + head, :, :HEAD_DIM] * keep
            total = both[:, HEAD_DIM:] + acc[2 * k + head, :, HEAD_DIM:] * keep
            put_part(columns[head], (number / total).astype(BF16))
            lses.append(top + jnp.log2(total))
        lane = lax.broadcasted_iota(jnp.int32, (ROWS, HEAD_DIM), 1)
        put_side(jnp.transpose(jnp.where(lane == 0, lses[0], lses[1]))[:8])

    def put(ref, index):
        def store(cols, value):
            ref[index, :, cols] = value
        return store

    def put_all(ref, index):
        def store(value):
            ref[index] = value
        return store

    def send_part(k):
        exchange(part_out.at[k], parts.at[local], (psend, precv), k, peers[k])
        exchange(side_out.at[k], sides.at[local], (psend, precv), 4 + k, peers[k])

    attend_fresh(3, blocks[3], put(part_out, 3), put_all(side_out, 3))
    attend_fresh(2, blocks[2], put(part_out, 2), put_all(side_out, 2))
    send_part(3)
    attend_fresh(1, blocks[1], put(part_out, 1), put_all(side_out, 1))
    send_part(2)
    attend_fresh(0, blocks[0], put(parts, local), put_all(sides, local))
    send_part(1)
    exchange(fresh_all.at[local], fresh_all.at[local], (gsend, grecv), 5, peers[2])
    for k in (3, 2, 1):
        arrived(parts.at[blocks[k]], (psend, precv), k, peers[k])
        arrived(sides.at[blocks[k]], (psend, precv), 4 + k, peers[k])
    stats = [sides[k] for k in range(4)]
    top = functools.reduce(jnp.maximum, stats)
    shares = [jnp.exp2(stat - top) for stat in stats]
    total = functools.reduce(jnp.add, shares)
    shares = [jnp.transpose(jnp.concatenate([share / total] * 16, axis=0)) for share in shares]
    for head in range(2):
        terms = [parts[k, :, columns[head]].astype(F32) * shares[k][:, head:head + 1] for k in range(4)]
        mine[:, columns[head]] = functools.reduce(jnp.add, terms).astype(BF16)
    tokens.finish()
    finals = TpGather(p, mine, att, local_sem.at[2, 1], tsend, trecv)
    finals.begin()
    for k in range(2):
        for h in range(2):
            fresh[2 * k + h, :PAD] = jnp.zeros((PAD, HEAD_DIM), F32)
            fresh[2 * k + h, PAD + SPAN:] = jnp.zeros((PAD, HEAD_DIM), F32)
    arrived(fresh_all.at[blocks[1]], (gsend, grecv), 4, peers[1])
    exchange(fresh_all.at[blocks[1]], fresh_all.at[blocks[1]], (gsend, grecv), 6, peers[2])
    finals.near()
    arrived(fresh_all.at[blocks[2]], (gsend, grecv), 5, peers[2])
    finals.far()
    arrived(fresh_all.at[blocks[3]], (gsend, grecv), 6, peers[2])
    stores = []
    for k, (rows_of, out) in enumerate(((keys, keys_out), (values, values_out))):
        for h in range(2):
            for block in range(4):
                begin = PAD + block * ROWS
                fresh[2 * k + h, begin:begin + ROWS] = fresh_all[block, k, :, columns[h]].astype(F32)

        for chunk in range(SLOTS // ROWS):
            begin = jnp.clip(first + chunk * ROWS, -ROWS, SPAN)
            place = lax.broadcasted_iota(jnp.int32, (ROWS, HEAD_DIM), 0) + begin
            inside = (place >= 0) & (place < SPAN)
            span = slice(chunk * ROWS, (chunk + 1) * ROWS)
            for h in range(2):
                new = fresh[2 * k + h, pl.ds(begin + PAD, ROWS), :]
                old = rows_of[span, columns[h]].astype(F32)
                rows_of[span, columns[h]] = jnp.where(inside, new, old).astype(BF16)
        stores.append(pltpu.make_async_copy(rows_of, out, load_sem.at[7 + k]))
        stores[-1].start()
    finals.rest()

    def out_rows(seqs):
        places = [(q // (NY * NZ), (q // NZ) % NY, q % NZ) for q in seqs]
        return jnp.concatenate([rb[place + (2 + k,)] for place in places for k in (0, 1)], axis=0)

    result = None
    for t in range(TP):
        rows = out_rows(range(t, 64, TP))
        term = lax.dot_general(att[t], rows, nt, preferred_element_type=F32)
        result = term if result is None else result + term
    out_ref[...] = (result + out_bias[...]).astype(BF16)
    for copy in stores:
        copy.wait()
    for copy in sent:
        copy.wait_send()
    for who in (q_gather, rest, finals):
        who.finish()


def hand_over_kernel(mixed, keys, values, mixed_out, keys_out, values_out, a, b, c, in_sem, out_sem):
    copies = []
    for src, mid, dst, count in ((mixed, a, mixed_out, 1), (keys, b, keys_out, 4), (values, c, values_out, 4)):
        rows = src.shape[0] // count
        for k in range(count):
            span = pl.ds(k * rows, rows)
            index = len(copies)
            copies.append((
                pltpu.make_async_copy(src.at[span], mid.at[span], in_sem.at[index]),
                pltpu.make_async_copy(mid.at[span], dst.at[span], out_sem.at[index]),
            ))
    for first, _ in copies:
        first.start()
    for first, second in copies:
        first.wait()
        second.start()
    for _, second in copies:
        second.wait()


def round_bf16(value):
    return np.asarray(np.asarray(value, np.float32).astype(jnp.bfloat16), np.float64)


def bias_table():
    table = np.zeros((HEADS, 1, HEAD_DIM), np.float64)
    for head in range(HEADS):
        slope = 2.0 ** (-8.0 * (head + 1) / HEADS) * LOG2E
        for column, value in ((0, slope * 128.0), (3, slope)):
            rest = value
            for k in range(3):
                table[head, 0, column + k] = round_bf16(rest)
                rest = rest - table[head, 0, column + k]
        table[head, 0, 6] = 1.0
    return table.astype(np.float32)


def dma(*count):
    return pltpu.SemaphoreType.DMA(count)


def on_device(
    hidden_in, norm_gain, norm_bias, qkv_weight, qkv_bias, out_weight, out_bias, key_cache, value_cache, cached_len,
):
    any_spec = pl.BlockSpec(memory_space=pl.ANY)

    def vm(*shape, dtype=BF16):
        return pltpu.VMEM(shape, dtype)

    results = pl.pallas_call(
        layer_kernel,
        name="layer",
        out_shape=(
            jax.ShapeDtypeStruct((ROWS, ROWS), BF16),
            jax.ShapeDtypeStruct((SLOTS, ROWS), BF16),
            jax.ShapeDtypeStruct((SLOTS, ROWS), BF16),
        ),
        in_specs=[SMEM_SPEC] + [any_spec] * 10,
        out_specs=(VMEM_SPEC, any_spec, any_spec),
        scratch_shapes=[
            vm(4, 2, ROWS, ROWS), vm(4, SPAN + 2 * PAD, HEAD_DIM, dtype=F32),
            vm(TP, ROWS, ROWS), vm(TP, ROWS, ROWS),
            vm(NY, NX, NZ, 16, ROWS), vm(NX, NY, NZ, 16, ROWS),
            vm(NY, NX, NZ, 2, 16, ROWS), vm(NX, NY, NZ, 4, 16, ROWS),
            vm(1, TP * ROWS, dtype=F32), vm(1, TP * ROWS, dtype=F32), vm(3, ROWS, dtype=F32), vm(1, ROWS, dtype=F32),
            vm(2, 1, HEAD_DIM, dtype=F32), vm(SLOTS, ROWS), vm(SLOTS, ROWS),
            vm(2, SLOTS, ROWS), vm(2, SLOTS, ROWS), vm(2, ROWS, ROWS), vm(2, ROWS, ROWS),
            vm(4, ROWS, ROWS), vm(8, ROWS, ROWS, dtype=F32), vm(8, ROWS, HEAD_DIM, dtype=F32),
            vm(4, ROWS, ROWS), vm(4, 8, ROWS, dtype=F32), vm(4, ROWS, ROWS), vm(4, 8, ROWS, dtype=F32),
            vm(ROWS, ROWS), vm(TP, ROWS, ROWS),
            dma(9), dma(3, 2), dma(6), dma(2, 2), dma(2, 2), dma(2, N_EDGES), dma(2, N_EDGES),
            dma(8), dma(8), dma(7), dma(7), dma(8), dma(8), dma(8), dma(8),
        ],
        compiler_params=pltpu.CompilerParams(collective_id=0, has_side_effects=True, vmem_limit_bytes=56 << 20),
    )(
        cached_len, hidden_in, norm_gain.reshape(1, TP * ROWS), norm_bias.reshape(1, TP * ROWS),
        qkv_weight, qkv_bias, out_weight.T, out_bias.reshape(1, ROWS), key_cache, value_cache,
        jnp.asarray(bias_table()),
    )
    return pl.pallas_call(
        hand_over_kernel,
        name="hand_over",
        out_shape=tuple(jax.ShapeDtypeStruct(r.shape, r.dtype) for r in results),
        in_specs=[any_spec] * 3,
        out_specs=(any_spec,) * 3,
        scratch_shapes=[vm(ROWS, ROWS), vm(SLOTS, ROWS), vm(SLOTS, ROWS), dma(9), dma(9)],
    )(*results)


def solution(mesh):
    placed = (
        P("seq", "tp"),
        P(),
        P(),
        P(None, "seq", "tp"),
        P(None, "tp"),
        P("tp", "seq"),
        P("tp"),
        P("seq", "tp"),
        P("seq", "tp"),
        P(),
    )
    return jax.shard_map(
        on_device,
        mesh=mesh,
        in_specs=placed,
        out_specs=(P("seq", "tp"), P("seq", "tp"), P("seq", "tp")),
        check_vma=False,
    )
```

```python
import functools
import math

import jax
import jax.numpy as jnp
import numpy as np
from jax import lax
from jax.experimental import pallas as pl
from jax.experimental.pallas import tpu as pltpu
from jax.sharding import PartitionSpec as P

HEADS = 16
HEAD_DIM = 128
REQS = 16
SPAN = 1024
NX, NY, NZ = 4, 8, 2
TP = 8
ROWS = 256
PAD = ROWS + 32
SLOTS = 2304
LOG2E = 1.4426950408889634
MESH = pl.DeviceIdType.MESH
BF16 = jnp.bfloat16
F32 = jnp.float32
VMEM_SPEC = pl.BlockSpec(memory_space=pltpu.VMEM)
SMEM_SPEC = pl.BlockSpec(memory_space=pltpu.SMEM)


class Node:
    def __init__(self, tree, ox, oy, way, parent):
        self.tree, self.ox, self.oy, self.way, self.parent = tree, ox, oy, way, parent
        self.depth = 0 if parent is None else parent.depth + 1
        self.kids = []
        self.sem = None
        if parent is not None:
            parent.kids.append(self)

    def grow(self, axis, hops):
        return Node(self.tree, self.ox - hops * (axis == 0), self.oy - hops * (axis == 1), (axis, hops), self)


def deep_ring(start, axis, far_up):
    size = (NX, NY)[axis]
    nodes = []
    for sign in (1, -1):
        node = start
        for _ in range(size // 2 - (0 if (sign == 1) == far_up else 1)):
            node = node.grow(axis, sign)
            nodes.append(node)
    return nodes


def shallow_ring(start, axis, far_up):
    if axis == 0:
        return [start.grow(0, 1), start.grow(0, -1), start.grow(0, 2 if far_up else -2)]
    near = [start.grow(1, 1), start.grow(1, -1)]
    far = [start.grow(1, 3), start.grow(1, -3)]
    more = [near[0].grow(1, 1), near[1].grow(1, -1), far[0].grow(1, 1) if far_up else far[1].grow(1, -1)]
    return near + far + more


class Forest:
    def __init__(self, ring, trees):
        self.trees, self.roots, self.edges = trees, {}, []
        for tree in trees:
            root = Node(tree, 0, 0, None, None)
            nodes = [root] + ring(root, tree, True)
            for node in list(nodes):
                off = node.oy if tree else node.ox
                nodes += ring(node, 1 - tree, off % 2 == 0 if tree else off in (0, -1))
            self.roots[tree] = root
            self.edges += nodes[1:]
        for index, node in enumerate(self.edges):
            node.sem = index
        self.depth = max(node.depth for node in self.edges)
        order = sorted(self.edges, key=lambda n: (abs(n.way[1]), n.sem))
        self.levels = [[n for n in order if n.depth == d] for d in range(self.depth + 1)]


DEEP, SHALLOW, LAST = Forest(deep_ring, (0, 1)), Forest(shallow_ring, (0, 1)), Forest(shallow_ring, (1,))
N_EDGES = len(DEEP.edges)


class Place:
    def __init__(self):
        self.s = lax.axis_index("seq")
        self.t = lax.axis_index("tp")
        self.x = lax.div(self.s, NY * NZ)
        self.y = lax.rem(lax.div(self.s, NZ), NY)
        self.z = lax.rem(self.s, NZ)
        self.zh = lax.div(self.t, 2)
        self.core = lax.rem(self.t, 2)

    def seq(self, x, y, z):
        return (x * NY + y) * NZ + z

    def beside(self, axis, sign):
        if axis == 0:
            return (self.seq(lax.rem(self.x + sign + NX, NX), self.y, self.z), self.t)
        return (self.seq(self.x, lax.rem(self.y + sign + NY, NY), self.z), self.t)

    def z_partner(self):
        return (self.seq(self.x, self.y, 1 - self.z), self.t)

    def y_partner(self):
        return (self.seq(self.x, self.y + 1 - 2 * lax.rem(self.y, 2), self.z), self.t)

    def diagonal(self):
        return (self.seq(self.x, self.y + 1 - 2 * lax.rem(self.y, 2), 1 - self.z), self.t)

    def core_partner(self):
        return (self.s, self.zh * 2 + 1 - self.core)

    def up(self, hops):
        return (self.s, lax.rem(self.zh + hops + 4, 4) * 2 + self.core)

    def piece(self, bufs, node):
        ax = lax.rem(self.x + node.ox + NX, NX)
        ay = lax.rem(self.y + node.oy + NY, NY)
        if node.tree == 0:
            return bufs[0].at[ay, ax]
        return bufs[1].at[ax, ay]


def remote(src, dst, send_sem, recv_sem, device):
    return pltpu.make_async_remote_copy(
        src_ref=src, dst_ref=dst, send_sem=send_sem, recv_sem=recv_sem,
        device_id=device, device_id_type=MESH,
    )


class Gather:
    def __init__(self, place, forest, halves, bufs, local_sem, zsend, zrecv, send, recv):
        self.p, self.forest, self.halves, self.bufs = place, forest, halves, bufs
        self.local_sem, self.zsend, self.zrecv, self.send, self.recv = local_sem, zsend, zrecv, send, recv
        self.sent = []

    def own(self, k):
        p = self.p
        return self.bufs[0].at[p.y, p.x, p.z] if k == 0 else self.bufs[1].at[p.x, p.y, p.z]

    def other(self, k):
        p = self.p
        return self.bufs[0].at[p.y, p.x, 1 - p.z] if k == 0 else self.bufs[1].at[p.x, p.y, 1 - p.z]

    def begin(self):
        self.locals = []
        for k in self.forest.trees:
            src = self.own(k) if self.halves is None else self.halves[k]
            copy = remote(src, self.own(k), self.zsend.at[k], self.zrecv.at[k], self.p.z_partner())
            copy.start()
            self.sent.append(copy)
        if self.halves is None:
            return
        for k in self.forest.trees:
            copy = pltpu.make_async_copy(self.halves[k], self.own(k), self.local_sem.at[k])
            copy.start()
            self.locals.append(copy)

    def forward(self, node):
        for kid in node.kids:
            piece = self.p.piece(self.bufs, node)
            copy = remote(piece, piece, self.send.at[kid.sem], self.recv.at[kid.sem], self.p.beside(*kid.way))
            copy.start()
            self.sent.append(copy)

    def roots(self):
        for k in self.forest.trees:
            if self.locals:
                self.locals[k].wait()
            other = self.other(k)
            remote(other, other, self.zsend.at[k], self.zrecv.at[k], self.p.z_partner()).wait_recv()
            self.forward(self.forest.roots[k])

    def take(self, node):
        piece = self.p.piece(self.bufs, node)
        way = (node.way[0], -node.way[1])
        remote(piece, piece, self.send.at[node.sem], self.recv.at[node.sem], self.p.beside(*way)).wait_recv()
        self.forward(node)

    def step(self, depth):
        for node in self.forest.levels[depth]:
            self.take(node)

    def finish(self):
        for copy in self.sent:
            copy.wait_send()


class TpGather:
    def __init__(self, place, src, buf, local_sem, send, recv):
        self.p, self.src, self.buf = place, src, buf
        self.local_sem, self.send, self.recv = local_sem, send, recv
        self.sent = []

    def block(self, hops, mine=True):
        p = self.p
        core = p.core if mine else 1 - p.core
        return self.buf.at[lax.rem(p.zh + hops + 4, 4) * 2 + core]

    def copy(self, src, dst, index, device):
        return remote(src, dst, self.send.at[index], self.recv.at[index], device)

    def start(self, src, dst, index, device):
        copy = self.copy(src, dst, index, device)
        copy.start()
        self.sent.append(copy)

    def begin(self):
        p = self.p
        half = ROWS // 2
        lower, upper = pl.ds(0, half), pl.ds(half, half)
        mine = self.block(0)
        self.start(self.src.at[lower], mine.at[lower], 0, p.up(1))
        self.start(self.src.at[upper], mine.at[upper], 1, p.up(-1))
        self.start(self.src.at[upper], mine.at[upper], 8, p.up(1))
        self.start(self.src.at[lower], mine.at[lower], 9, p.up(-1))
        self.start(self.src, mine, 4, p.core_partner())
        self.local = pltpu.make_async_copy(self.src, mine, self.local_sem)
        self.local.start()

    def near(self):
        p = self.p
        half = ROWS // 2
        lower, upper = pl.ds(0, half), pl.ds(half, half)
        low, high = self.block(-1), self.block(1)
        self.copy(low.at[lower], low.at[lower], 0, p.up(-1)).wait_recv()
        self.start(low.at[lower], low.at[lower], 2, p.up(1))
        self.copy(high.at[upper], high.at[upper], 1, p.up(1)).wait_recv()
        self.start(high.at[upper], high.at[upper], 3, p.up(-1))
        self.copy(low.at[upper], low.at[upper], 8, p.up(-1)).wait_recv()
        self.start(low, low, 5, p.core_partner())
        self.copy(high.at[lower], high.at[lower], 9, p.up(1)).wait_recv()
        self.start(high, high, 6, p.core_partner())

    def far(self):
        p = self.p
        half = ROWS // 2
        block = self.block(2)
        lower, upper = block.at[pl.ds(0, half)], block.at[pl.ds(half, half)]
        self.copy(lower, lower, 2, p.up(-1)).wait_recv()
        self.copy(upper, upper, 3, p.up(1)).wait_recv()
        self.start(block, block, 7, p.core_partner())

    def rest(self):
        self.local.wait()
        for index, hops in ((4, 0), (5, -1), (6, 1), (7, 2)):
            block = self.block(hops, mine=False)
            self.copy(block, block, index, self.p.core_partner()).wait_recv()

    def finish(self):
        for copy in self.sent:
            copy.wait_send()


def layer_kernel(
    length_ref, hidden_hbm, gain_hbm, shift_hbm, weight_hbm, bias_hbm, out_weight_hbm, out_bias_hbm,
    keys_hbm, values_hbm, table_hbm,
    out_ref, keys_out, values_out,
    fresh_all, fresh, hid, norm, qa, qb, ka, kb, ob, gain, shift, bias, out_bias, table, keys, values,
    kaug, vaug, kfresh, vfresh, queries, acc, tops, parts, sides, part_out, side_out, mine, att,
    load_sem, local_sem, move_sem, zsend, zrecv, send, recv, hsend, hrecv, gsend, grecv, psend, precv, tsend, trecv,
):
    p = Place()
    peers = [None, p.z_partner(), p.y_partner(), p.diagonal()]
    local = lax.rem(p.s, 4)
    target_seq = lax.rem(p.s, 8) * 8 + p.t
    target = (target_seq, lax.div(p.s, 8))
    source = (p.t * 8 + lax.div(p.s, 8), lax.rem(p.s, 8))
    away = target_seq != p.s
    away = jnp.logical_or(away, target[1] != p.t)
    steady = peers[1:] + [p.core_partner(), p.up(1), p.up(-1),
                          p.beside(0, 1), p.beside(0, -1), p.beside(0, 2),
                          p.beside(1, 1), p.beside(1, -1), p.beside(1, 3), p.beside(1, -3)]
    barrier = pltpu.get_barrier_semaphore()
    for device in steady:
        pl.semaphore_signal(barrier, inc=1, device_id=device, device_id_type=MESH)

    @pl.when(away)
    def _():
        for device in (target, source):
            pl.semaphore_signal(barrier, inc=1, device_id=device, device_id_type=MESH)

    loads = {}
    for index, (name, src, dst) in enumerate((
        ("gain", gain_hbm, gain), ("shift", shift_hbm, shift), ("bias", bias_hbm, bias),
        ("out_bias", out_bias_hbm, out_bias), ("table", table_hbm.at[pl.ds(p.t * 2, 2)], table),
        ("keys", keys_hbm, keys), ("values", values_hbm, values),
    )):
        loads[name] = pltpu.make_async_copy(src, dst, load_sem.at[index])
        loads[name].start()

    pl.semaphore_wait(barrier, len(steady) + 2 * away.astype(jnp.int32))

    def gather(index, forest, halves, bufs):
        return Gather(p, forest, halves, bufs, local_sem.at[index], zsend.at[index], zrecv.at[index],
                      send.at[index], recv.at[index])

    lower, upper = pl.ds(0, 16), pl.ds(16, 16)
    q_gather = gather(0, SHALLOW, [weight_hbm.at[0, lower], weight_hbm.at[0, upper]], (qa, qb))
    kv_gather = gather(1, DEEP, None, (ka, kb))
    o_gather = gather(2, LAST, None, (None, ob))
    tokens = TpGather(p, hidden_hbm, hid, local_sem.at[2, 0], hsend, hrecv)
    placed = [
        pltpu.make_async_copy(weight_hbm.at[index, rows], place, local_sem.at[1, k])
        for k, (index, rows, place) in enumerate((
            (1, lower, kv_gather.own(0).at[0]), (1, upper, kv_gather.own(1).at[0]),
            (2, lower, kv_gather.own(1).at[1]), (2, upper, kv_gather.own(1).at[2]),
        ))
    ]
    for copy in placed:
        copy.start()
    q_gather.begin()
    tokens.begin()
    for copy in placed:
        copy.wait()
    kv_gather.begin()

    tx, ty, tz = lax.div(target_seq, 16), lax.rem(lax.div(target_seq, 2), NY), lax.rem(target_seq, 2)
    pieces = [out_weight_hbm.at[lower], out_weight_hbm.at[upper]]
    places = [ob.at[tx, ty, tz, k] for k in (0, 1)]
    moved = [remote(pieces[k], places[k], move_sem.at[k], move_sem.at[2 + k], target) for k in (0, 1)]
    stay = [pltpu.make_async_copy(pieces[k], places[k], move_sem.at[4 + k]) for k in (0, 1)]

    @pl.when(away)
    def _():
        for copy in moved:
            copy.start()

    @pl.when(jnp.logical_not(away))
    def _():
        for copy in stay:
            copy.start()

    q_gather.roots()
    kv_gather.roots()

    length = length_ref[lax.div(p.s, 4)]
    first = local * SLOTS - length

    def aux(count, start, cached):
        place = lax.broadcasted_iota(jnp.int32, (count, HEAD_DIM), 0) + start
        lane = lax.broadcasted_iota(jnp.int32, (count, HEAD_DIM), 1)
        high = lax.shift_right_arithmetic(place, 7)
        low = place - high * 128
        number = jnp.where(lane < 3, high, jnp.where(lane < 6, low, 0)).astype(F32)
        if cached:
            number = jnp.where(place >= 0, jnp.where(lane == 6, -1e30, 0.0), number)
        return number.astype(BF16)

    def ones(count):
        return jnp.ones((count, HEAD_DIM), BF16)

    columns = [slice(0, HEAD_DIM), slice(HEAD_DIM, 2 * HEAD_DIM)]

    def prepare_keys():
        loads["keys"].wait()
        number = aux(SLOTS, first, True)
        alive = lax.broadcasted_iota(jnp.int32, (SLOTS, HEAD_DIM), 0) + first < 0
        for head in range(2):
            kaug[head, :, :HEAD_DIM] = jnp.where(alive, keys[:, columns[head]].astype(F32), 0.0).astype(BF16)
            kaug[head, :, HEAD_DIM:] = number

    def prepare_values():
        loads["values"].wait()
        for head in range(2):
            vaug[head, :, :HEAD_DIM] = values[:, columns[head]]
            vaug[head, :, HEAD_DIM:] = ones(SLOTS)

    def normalise(start, rows):
        numbers = [hid[t, start:start + rows, :].astype(F32) for t in range(TP)]
        mean = jnp.sum(functools.reduce(jnp.add, numbers), axis=1, keepdims=True) * (1.0 / (TP * ROWS))
        numbers = [v - mean for v in numbers]
        squares = functools.reduce(jnp.add, [v * v for v in numbers])
        variance = jnp.sum(squares, axis=1, keepdims=True) * (1.0 / (TP * ROWS))
        scale = lax.rsqrt(variance + 1e-05)
        for t in range(TP):
            cols = slice(t * ROWS, (t + 1) * ROWS)
            norm[t, start:start + rows, :] = (numbers[t] * scale * gain[:, cols] + shift[:, cols]).astype(BF16)

    def places(seqs):
        return [(q // (NY * NZ), (q // NZ) % NY, q % NZ) for q in seqs]

    def q_rows(seqs):
        return [ref for x, y, z in places(seqs) for ref in (qa[y, x, z], qb[x, y, z])]

    def k_rows(seqs):
        return [ref for x, y, z in places(seqs) for ref in (ka[y, x, z, 0], kb[x, y, z, 0])]

    def v_rows(seqs):
        return [ref for x, y, z in places(seqs) for ref in (kb[x, y, z, 1], kb[x, y, z, 2])]

    def out_rows(seqs):
        return [ref for x, y, z in places(seqs) for ref in (ob[x, y, z, 0], ob[x, y, z, 1])]

    def project(rows_of, row):
        total = None
        for t in range(TP):
            rows = jnp.concatenate(rows_of(range(t * 8, t * 8 + 8)), axis=0)
            part = jnp.dot(norm[t], rows, preferred_element_type=F32)
            total = part if total is None else total + part
        return total + bias[row:row + 1, :]

    prepare_keys()
    q_gather.step(1)
    tokens.near()
    kv_gather.step(1)
    prepare_values()
    q_gather.step(2)
    tokens.far()
    kv_gather.step(2)
    q_gather.step(3)

    @pl.when(away)
    def _():
        for k in (0, 1):
            own = ob.at[p.x, p.y, p.z, k]
            remote(own, own, move_sem.at[k], move_sem.at[2 + k], source).wait_recv()
            moved[k].wait_send()

    @pl.when(jnp.logical_not(away))
    def _():
        for copy in stay:
            copy.wait()

    o_gather.begin()
    for name in ("gain", "shift", "bias", "out_bias", "table"):
        loads[name].wait()
    tokens.rest()
    normalise(0, 128)
    normalise(128, 128)
    queries[local] = (project(q_rows, 0) * (LOG2E / math.sqrt(HEAD_DIM))).astype(BF16)
    sent = []

    def exchange(src, dst, sems, index, peer):
        copy = remote(src, dst, sems[0].at[index], sems[1].at[index], peer)
        copy.start()
        sent.append(copy)

    def arrived(dst, sems, index, peer):
        remote(dst, dst, sems[0].at[index], sems[1].at[index], peer).wait_recv()

    for k in (1, 2, 3):
        exchange(queries.at[local], queries.at[local], (gsend, grecv), k, peers[k])

    def query_of(block, head):
        side = jnp.broadcast_to(table[head], (ROWS, HEAD_DIM)).astype(BF16)
        return jnp.concatenate([queries[block, :, columns[head]], side], axis=1)

    nt = (((1,), (1,)), ((), ()))

    def attend(k, block):
        for head in range(2):
            score = lax.dot_general(query_of(block, head), kaug[head], nt, preferred_element_type=F32)
            top = jnp.max(score, axis=1, keepdims=True)
            weight = jnp.exp2(score - top).astype(BF16)
            acc[2 * k + head] = jnp.dot(weight, vaug[head], preferred_element_type=F32)
            tops[2 * k + head] = jnp.broadcast_to(top, (ROWS, HEAD_DIM))

    blocks = [local] + [lax.rem(peer[0], 4) for peer in peers[1:]]
    kv_gather.step(3)
    attend(0, blocks[0])
    kv_gather.step(4)
    arrived(queries.at[blocks[1]], (gsend, grecv), 1, peers[1])
    attend(1, blocks[1])
    kv_gather.step(5)
    arrived(queries.at[blocks[2]], (gsend, grecv), 2, peers[2])
    attend(2, blocks[2])
    kv_gather.step(6)
    o_gather.roots()
    for which, rows_of in ((0, k_rows), (1, v_rows)):
        fresh_all[local, which] = project(rows_of, 1 + which).astype(BF16)
        if which == 0:
            exchange(fresh_all.at[local, 0], fresh_all.at[local, 0], (gsend, grecv), 4, peers[1])
            exchange(fresh_all.at[local, 0], fresh_all.at[local, 0], (gsend, grecv), 5, peers[2])
    number = aux(ROWS, local * ROWS, False)
    for head in range(2):
        kfresh[head, :, :HEAD_DIM] = fresh_all[local, 0, :, columns[head]]
        kfresh[head, :, HEAD_DIM:] = number
        vfresh[head, :, :HEAD_DIM] = fresh_all[local, 1, :, columns[head]]
        vfresh[head, :, HEAD_DIM:] = ones(ROWS)

    def attend_fresh(k, block, put_part, put_side):
        row = lax.broadcasted_iota(jnp.int32, (ROWS, ROWS), 0) + block * ROWS
        column = lax.broadcasted_iota(jnp.int32, (ROWS, ROWS), 1) + local * ROWS
        lses = []
        for head in range(2):
            score = lax.dot_general(query_of(block, head), kfresh[head], nt, preferred_element_type=F32)
            score = jnp.where(column <= row, score, -1e30)
            before = tops[2 * k + head]
            top = jnp.maximum(before, jnp.max(score, axis=1, keepdims=True))
            weight = jnp.exp2(score - jnp.concatenate([top, top], axis=1)).astype(BF16)
            keep = jnp.exp2(before - top)
            both = jnp.dot(weight, vfresh[head], preferred_element_type=F32)
            number = both[:, :HEAD_DIM] + acc[2 * k + head, :, :HEAD_DIM] * keep
            total = both[:, HEAD_DIM:] + acc[2 * k + head, :, HEAD_DIM:] * keep
            put_part(columns[head], (number / total).astype(BF16))
            lses.append(top + jnp.log2(total))
        lane = lax.broadcasted_iota(jnp.int32, (ROWS, HEAD_DIM), 1)
        put_side(jnp.transpose(jnp.where(lane == 0, lses[0], lses[1]))[:8])

    def put(ref, index):
        def store(cols, value):
            ref[index, :, cols] = value
        return store

    def put_all(ref, index):
        def store(value):
            ref[index] = value
        return store

    def send_part(k):
        exchange(part_out.at[k], parts.at[local], (psend, precv), k, peers[k])
        exchange(side_out.at[k], sides.at[local], (psend, precv), 4 + k, peers[k])

    attend_fresh(1, blocks[1], put(part_out, 1), put_all(side_out, 1))
    attend_fresh(2, blocks[2], put(part_out, 2), put_all(side_out, 2))
    send_part(1)
    arrived(queries.at[blocks[3]], (gsend, grecv), 3, peers[3])
    send_part(2)
    attend(3, blocks[3])
    attend_fresh(3, blocks[3], put(part_out, 3), put_all(side_out, 3))
    attend_fresh(0, blocks[0], put(parts, local), put_all(sides, local))
    send_part(3)
    exchange(fresh_all.at[local, 1], fresh_all.at[local, 1], (gsend, grecv), 6, peers[1])
    exchange(fresh_all.at[local, 1], fresh_all.at[local, 1], (gsend, grecv), 7, peers[2])
    key_block = fresh_all.at[blocks[1], 0]
    arrived(key_block, (gsend, grecv), 4, peers[1])
    exchange(key_block, key_block, (gsend, grecv), 8, peers[2])
    o_gather.step(1)
    for k in (1, 2, 3):
        arrived(parts.at[blocks[k]], (psend, precv), k, peers[k])
        arrived(sides.at[blocks[k]], (psend, precv), 4 + k, peers[k])
    stats = [sides[k] for k in range(4)]
    top = functools.reduce(jnp.maximum, stats)
    shares = [jnp.exp2(stat - top) for stat in stats]
    total = functools.reduce(jnp.add, shares)
    shares = [jnp.transpose(jnp.concatenate([share / total] * 16, axis=0)) for share in shares]
    for head in range(2):
        terms = [parts[k, :, columns[head]].astype(F32) * shares[k][:, head:head + 1] for k in range(4)]
        mine[:, columns[head]] = functools.reduce(jnp.add, terms).astype(BF16)
    tokens.finish()
    finals = TpGather(p, mine, att, local_sem.at[2, 1], tsend, trecv)
    finals.begin()
    for k in range(2):
        for h in range(2):
            fresh[2 * k + h, :PAD] = jnp.zeros((PAD, HEAD_DIM), F32)
            fresh[2 * k + h, PAD + SPAN:] = jnp.zeros((PAD, HEAD_DIM), F32)
    finals.near()
    o_gather.step(2)
    value_block = fresh_all.at[blocks[1], 1]
    arrived(value_block, (gsend, grecv), 6, peers[1])
    exchange(value_block, value_block, (gsend, grecv), 9, peers[2])
    finals.far()
    arrived(fresh_all.at[blocks[2], 0], (gsend, grecv), 5, peers[2])
    arrived(fresh_all.at[blocks[2], 1], (gsend, grecv), 7, peers[2])
    arrived(fresh_all.at[blocks[3], 0], (gsend, grecv), 8, peers[2])
    arrived(fresh_all.at[blocks[3], 1], (gsend, grecv), 9, peers[2])
    stores = []
    for k, (rows_of, out) in enumerate(((keys, keys_out), (values, values_out))):
        for h in range(2):
            for block in range(4):
                begin = PAD + block * ROWS
                fresh[2 * k + h, begin:begin + ROWS] = fresh_all[block, k, :, columns[h]].astype(F32)

        for chunk in range(SLOTS // ROWS):
            begin = jnp.clip(first + chunk * ROWS, -ROWS, SPAN)
            place = lax.broadcasted_iota(jnp.int32, (ROWS, HEAD_DIM), 0) + begin
            inside = (place >= 0) & (place < SPAN)
            span = slice(chunk * ROWS, (chunk + 1) * ROWS)
            for h in range(2):
                new = fresh[2 * k + h, pl.ds(begin + PAD, ROWS), :]
                old = rows_of[span, columns[h]].astype(F32)
                rows_of[span, columns[h]] = jnp.where(inside, new, old).astype(BF16)
        stores.append(pltpu.make_async_copy(rows_of, out, load_sem.at[7 + k]))
        stores[-1].start()
    o_gather.step(3)
    finals.rest()

    result = None
    for t in range(TP):
        rows = jnp.concatenate(out_rows(range(t, 64, TP)), axis=0)
        term = lax.dot_general(att[t], rows, nt, preferred_element_type=F32)
        result = term if result is None else result + term
    out_ref[...] = (result + out_bias[...]).astype(BF16)
    for copy in stores:
        copy.wait()
    for copy in sent:
        copy.wait_send()
    for who in (q_gather, kv_gather, o_gather, finals):
        who.finish()


def hand_over_kernel(mixed, keys, values, mixed_out, keys_out, values_out, a, b, c, in_sem, out_sem):
    copies = []
    for src, mid, dst, count in ((mixed, a, mixed_out, 1), (keys, b, keys_out, 4), (values, c, values_out, 4)):
        rows = src.shape[0] // count
        for k in range(count):
            span = pl.ds(k * rows, rows)
            index = len(copies)
            copies.append((
                pltpu.make_async_copy(src.at[span], mid.at[span], in_sem.at[index]),
                pltpu.make_async_copy(mid.at[span], dst.at[span], out_sem.at[index]),
            ))
    for first, _ in copies:
        first.start()
    for first, second in copies:
        first.wait()
        second.start()
    for _, second in copies:
        second.wait()


def round_bf16(value):
    return np.asarray(np.asarray(value, np.float32).astype(jnp.bfloat16), np.float64)


def bias_table():
    table = np.zeros((HEADS, 1, HEAD_DIM), np.float64)
    for head in range(HEADS):
        slope = 2.0 ** (-8.0 * (head + 1) / HEADS) * LOG2E
        for column, value in ((0, slope * 128.0), (3, slope)):
            rest = value
            for k in range(3):
                table[head, 0, column + k] = round_bf16(rest)
                rest = rest - table[head, 0, column + k]
        table[head, 0, 6] = 1.0
    return table.astype(np.float32)


def dma(*count):
    return pltpu.SemaphoreType.DMA(count)


def on_device(
    hidden_in, norm_gain, norm_bias, qkv_weight, qkv_bias, out_weight, out_bias, key_cache, value_cache, cached_len,
):
    any_spec = pl.BlockSpec(memory_space=pl.ANY)

    def vm(*shape, dtype=BF16):
        return pltpu.VMEM(shape, dtype)

    results = pl.pallas_call(
        layer_kernel,
        name="layer",
        out_shape=(
            jax.ShapeDtypeStruct((ROWS, ROWS), BF16),
            jax.ShapeDtypeStruct((SLOTS, ROWS), BF16),
            jax.ShapeDtypeStruct((SLOTS, ROWS), BF16),
        ),
        in_specs=[SMEM_SPEC] + [any_spec] * 10,
        out_specs=(VMEM_SPEC, any_spec, any_spec),
        scratch_shapes=[
            vm(4, 2, ROWS, ROWS), vm(4, SPAN + 2 * PAD, HEAD_DIM, dtype=F32),
            vm(TP, ROWS, ROWS), vm(TP, ROWS, ROWS),
            vm(NY, NX, NZ, 16, ROWS), vm(NX, NY, NZ, 16, ROWS),
            vm(NY, NX, NZ, 1, 16, ROWS), vm(NX, NY, NZ, 3, 16, ROWS), vm(NX, NY, NZ, 2, 16, ROWS),
            vm(1, TP * ROWS, dtype=F32), vm(1, TP * ROWS, dtype=F32), vm(3, ROWS, dtype=F32), vm(1, ROWS, dtype=F32),
            vm(2, 1, HEAD_DIM, dtype=F32), vm(SLOTS, ROWS), vm(SLOTS, ROWS),
            vm(2, SLOTS, ROWS), vm(2, SLOTS, ROWS), vm(2, ROWS, ROWS), vm(2, ROWS, ROWS),
            vm(4, ROWS, ROWS), vm(8, ROWS, ROWS, dtype=F32), vm(8, ROWS, HEAD_DIM, dtype=F32),
            vm(4, ROWS, ROWS), vm(4, 8, ROWS, dtype=F32), vm(4, ROWS, ROWS), vm(4, 8, ROWS, dtype=F32),
            vm(ROWS, ROWS), vm(TP, ROWS, ROWS),
            dma(9), dma(3, 4), dma(6), dma(3, 2), dma(3, 2), dma(3, N_EDGES), dma(3, N_EDGES),
            dma(10), dma(10), dma(10), dma(10), dma(8), dma(8), dma(10), dma(10),
        ],
        compiler_params=pltpu.CompilerParams(collective_id=0, has_side_effects=True, vmem_limit_bytes=56 << 20),
    )(
        cached_len, hidden_in, norm_gain.reshape(1, TP * ROWS), norm_bias.reshape(1, TP * ROWS),
        qkv_weight, qkv_bias, out_weight.T, out_bias.reshape(1, ROWS), key_cache, value_cache,
        jnp.asarray(bias_table()),
    )
    return pl.pallas_call(
        hand_over_kernel,
        name="hand_over",
        out_shape=tuple(jax.ShapeDtypeStruct(r.shape, r.dtype) for r in results),
        in_specs=[any_spec] * 3,
        out_specs=(any_spec,) * 3,
        scratch_shapes=[vm(ROWS, ROWS), vm(SLOTS, ROWS), vm(SLOTS, ROWS), dma(9), dma(9)],
    )(*results)


def solution(mesh):
    placed = (
        P("seq", "tp"),
        P(),
        P(),
        P(None, "seq", "tp"),
        P(None, "tp"),
        P("tp", "seq"),
        P("tp"),
        P("seq", "tp"),
        P("seq", "tp"),
        P(),
    )
    return jax.shard_map(
        on_device,
        mesh=mesh,
        in_specs=placed,
        out_specs=(P("seq", "tp"), P("seq", "tp"), P("seq", "tp")),
        check_vma=False,
    )
```

```python
import functools
import math

import jax
import jax.numpy as jnp
import numpy as np
from jax import lax
from jax.experimental import pallas as pl
from jax.experimental.pallas import tpu as pltpu
from jax.sharding import PartitionSpec as P

HEADS = 16
HEAD_DIM = 128
REQS = 16
SPAN = 1024
NX, NY, NZ = 4, 8, 2
TP = 8
ROWS = 256
PAD = ROWS + 32
SLOTS = 2304
LOG2E = 1.4426950408889634
MESH = pl.DeviceIdType.MESH
BF16 = jnp.bfloat16
F32 = jnp.float32
VMEM_SPEC = pl.BlockSpec(memory_space=pltpu.VMEM)
SMEM_SPEC = pl.BlockSpec(memory_space=pltpu.SMEM)


class Node:
    def __init__(self, tree, ox, oy, way, parent):
        self.tree, self.ox, self.oy, self.way, self.parent = tree, ox, oy, way, parent
        self.depth = 0 if parent is None else parent.depth + 1
        self.kids = []
        self.sem = None
        if parent is not None:
            parent.kids.append(self)

    def grow(self, axis, hops):
        return Node(self.tree, self.ox - hops * (axis == 0), self.oy - hops * (axis == 1), (axis, hops), self)


def deep_ring(start, axis, far_up):
    size = (NX, NY)[axis]
    nodes = []
    for sign in (1, -1):
        node = start
        for _ in range(size // 2 - (0 if (sign == 1) == far_up else 1)):
            node = node.grow(axis, sign)
            nodes.append(node)
    return nodes


def shallow_ring(start, axis, far_up):
    if axis == 0:
        return [start.grow(0, 1), start.grow(0, -1), start.grow(0, 2 if far_up else -2)]
    near = [start.grow(1, 1), start.grow(1, -1)]
    far = [start.grow(1, 3), start.grow(1, -3)]
    more = [near[0].grow(1, 1), near[1].grow(1, -1), far[0].grow(1, 1) if far_up else far[1].grow(1, -1)]
    return near + far + more


class Forest:
    def __init__(self, ring, trees):
        self.trees, self.roots, self.edges = trees, {}, []
        for tree in trees:
            root = Node(tree, 0, 0, None, None)
            nodes = [root] + ring(root, tree, True)
            for node in list(nodes):
                off = node.oy if tree else node.ox
                nodes += ring(node, 1 - tree, off % 2 == 0 if tree else off in (0, -1))
            self.roots[tree] = root
            self.edges += nodes[1:]
        for index, node in enumerate(self.edges):
            node.sem = index
        self.depth = max(node.depth for node in self.edges)
        order = sorted(self.edges, key=lambda n: (abs(n.way[1]), n.sem))
        self.levels = [[n for n in order if n.depth == d] for d in range(self.depth + 1)]


DEEP, SHALLOW, LAST = Forest(deep_ring, (0, 1)), Forest(shallow_ring, (0, 1)), Forest(shallow_ring, (1,))
N_EDGES = len(DEEP.edges)


class Place:
    def __init__(self):
        self.s = lax.axis_index("seq")
        self.t = lax.axis_index("tp")
        self.x = lax.div(self.s, NY * NZ)
        self.y = lax.rem(lax.div(self.s, NZ), NY)
        self.z = lax.rem(self.s, NZ)
        self.zh = lax.div(self.t, 2)
        self.core = lax.rem(self.t, 2)

    def seq(self, x, y, z):
        return (x * NY + y) * NZ + z

    def beside(self, axis, sign):
        if axis == 0:
            return (self.seq(lax.rem(self.x + sign + NX, NX), self.y, self.z), self.t)
        return (self.seq(self.x, lax.rem(self.y + sign + NY, NY), self.z), self.t)

    def z_partner(self):
        return (self.seq(self.x, self.y, 1 - self.z), self.t)

    def y_partner(self):
        return (self.seq(self.x, self.y + 1 - 2 * lax.rem(self.y, 2), self.z), self.t)

    def diagonal(self):
        return (self.seq(self.x, self.y + 1 - 2 * lax.rem(self.y, 2), 1 - self.z), self.t)

    def core_partner(self):
        return (self.s, self.zh * 2 + 1 - self.core)

    def up(self, hops):
        return (self.s, lax.rem(self.zh + hops + 4, 4) * 2 + self.core)

    def piece(self, bufs, node):
        ax = lax.rem(self.x + node.ox + NX, NX)
        ay = lax.rem(self.y + node.oy + NY, NY)
        if node.tree == 0:
            return bufs[0].at[ay, ax]
        return bufs[1].at[ax, ay]


def remote(src, dst, send_sem, recv_sem, device):
    return pltpu.make_async_remote_copy(
        src_ref=src, dst_ref=dst, send_sem=send_sem, recv_sem=recv_sem,
        device_id=device, device_id_type=MESH,
    )


class Gather:
    def __init__(self, place, forest, halves, bufs, local_sem, zsend, zrecv, send, recv):
        self.p, self.forest, self.halves, self.bufs = place, forest, halves, bufs
        self.local_sem, self.zsend, self.zrecv, self.send, self.recv = local_sem, zsend, zrecv, send, recv
        self.sent = []

    def own(self, k):
        p = self.p
        return self.bufs[0].at[p.y, p.x, p.z] if k == 0 else self.bufs[1].at[p.x, p.y, p.z]

    def other(self, k):
        p = self.p
        return self.bufs[0].at[p.y, p.x, 1 - p.z] if k == 0 else self.bufs[1].at[p.x, p.y, 1 - p.z]

    def begin(self):
        self.locals = []
        for k in self.forest.trees:
            src = self.own(k) if self.halves is None else self.halves[k]
            copy = remote(src, self.own(k), self.zsend.at[k], self.zrecv.at[k], self.p.z_partner())
            copy.start()
            self.sent.append(copy)
        if self.halves is None:
            return
        for k in self.forest.trees:
            copy = pltpu.make_async_copy(self.halves[k], self.own(k), self.local_sem.at[k])
            copy.start()
            self.locals.append(copy)

    def forward(self, node):
        for kid in node.kids:
            piece = self.p.piece(self.bufs, node)
            copy = remote(piece, piece, self.send.at[kid.sem], self.recv.at[kid.sem], self.p.beside(*kid.way))
            copy.start()
            self.sent.append(copy)

    def roots(self):
        for k in self.forest.trees:
            if self.locals:
                self.locals[k].wait()
            other = self.other(k)
            remote(other, other, self.zsend.at[k], self.zrecv.at[k], self.p.z_partner()).wait_recv()
            self.forward(self.forest.roots[k])

    def take(self, node):
        piece = self.p.piece(self.bufs, node)
        way = (node.way[0], -node.way[1])
        remote(piece, piece, self.send.at[node.sem], self.recv.at[node.sem], self.p.beside(*way)).wait_recv()
        self.forward(node)

    def step(self, depth):
        for node in self.forest.levels[depth]:
            self.take(node)

    def finish(self):
        for copy in self.sent:
            copy.wait_send()


class TpGather:
    def __init__(self, place, src, buf, local_sem, send, recv):
        self.p, self.src, self.buf = place, src, buf
        self.local_sem, self.send, self.recv = local_sem, send, recv
        self.sent = []

    def block(self, hops, mine=True):
        p = self.p
        core = p.core if mine else 1 - p.core
        return self.buf.at[lax.rem(p.zh + hops + 4, 4) * 2 + core]

    def copy(self, src, dst, index, device):
        return remote(src, dst, self.send.at[index], self.recv.at[index], device)

    def start(self, src, dst, index, device):
        copy = self.copy(src, dst, index, device)
        copy.start()
        self.sent.append(copy)

    def begin(self):
        p = self.p
        half = ROWS // 2
        lower, upper = pl.ds(0, half), pl.ds(half, half)
        mine = self.block(0)
        self.start(self.src.at[lower], mine.at[lower], 0, p.up(1))
        self.start(self.src.at[upper], mine.at[upper], 1, p.up(-1))
        self.start(self.src.at[upper], mine.at[upper], 8, p.up(1))
        self.start(self.src.at[lower], mine.at[lower], 9, p.up(-1))
        self.start(self.src, mine, 4, p.core_partner())
        self.local = pltpu.make_async_copy(self.src, mine, self.local_sem)
        self.local.start()

    def near(self):
        p = self.p
        half = ROWS // 2
        lower, upper = pl.ds(0, half), pl.ds(half, half)
        low, high = self.block(-1), self.block(1)
        self.copy(low.at[lower], low.at[lower], 0, p.up(-1)).wait_recv()
        self.start(low.at[lower], low.at[lower], 2, p.up(1))
        self.copy(high.at[upper], high.at[upper], 1, p.up(1)).wait_recv()
        self.start(high.at[upper], high.at[upper], 3, p.up(-1))
        self.copy(low.at[upper], low.at[upper], 8, p.up(-1)).wait_recv()
        self.start(low, low, 5, p.core_partner())
        self.copy(high.at[lower], high.at[lower], 9, p.up(1)).wait_recv()
        self.start(high, high, 6, p.core_partner())

    def far(self):
        p = self.p
        half = ROWS // 2
        block = self.block(2)
        lower, upper = block.at[pl.ds(0, half)], block.at[pl.ds(half, half)]
        self.copy(lower, lower, 2, p.up(-1)).wait_recv()
        self.copy(upper, upper, 3, p.up(1)).wait_recv()
        self.start(block, block, 7, p.core_partner())

    def rest(self):
        self.local.wait()
        for index, hops in ((4, 0), (5, -1), (6, 1), (7, 2)):
            block = self.block(hops, mine=False)
            self.copy(block, block, index, self.p.core_partner()).wait_recv()

    def finish(self):
        for copy in self.sent:
            copy.wait_send()


def layer_kernel(
    length_ref, hidden_hbm, gain_hbm, shift_hbm, weight_hbm, bias_hbm, out_weight_hbm, out_bias_hbm,
    keys_hbm, values_hbm, table_hbm,
    out_ref, keys_out, values_out,
    fresh_all, fresh, hid, norm, qa, qb, ka, kb, ob, gain, shift, bias, out_bias, table, keys, values,
    kaug, vaug, kfresh, vfresh, queries, acc, tops, parts, sides, part_out, side_out, mine, att,
    load_sem, local_sem, move_sem, zsend, zrecv, send, recv, hsend, hrecv, gsend, grecv, psend, precv, tsend, trecv,
):
    p = Place()
    peers = [None, p.z_partner(), p.y_partner(), p.diagonal()]
    local = lax.rem(p.s, 4)
    target_seq = lax.rem(p.s, 8) * 8 + p.t
    target = (target_seq, lax.div(p.s, 8))
    source = (p.t * 8 + lax.div(p.s, 8), lax.rem(p.s, 8))
    away = target_seq != p.s
    away = jnp.logical_or(away, target[1] != p.t)
    steady = peers[1:] + [p.core_partner(), p.up(1), p.up(-1),
                          p.beside(0, 1), p.beside(0, -1), p.beside(0, 2),
                          p.beside(1, 1), p.beside(1, -1), p.beside(1, 3), p.beside(1, -3)]
    barrier = pltpu.get_barrier_semaphore()
    for device in steady:
        pl.semaphore_signal(barrier, inc=1, device_id=device, device_id_type=MESH)

    @pl.when(away)
    def _():
        for device in (target, source):
            pl.semaphore_signal(barrier, inc=1, device_id=device, device_id_type=MESH)

    loads = {}
    for index, (name, src, dst) in enumerate((
        ("gain", gain_hbm, gain), ("shift", shift_hbm, shift), ("bias", bias_hbm, bias),
        ("out_bias", out_bias_hbm, out_bias), ("table", table_hbm.at[pl.ds(p.t * 2, 2)], table),
        ("keys", keys_hbm, keys), ("values", values_hbm, values),
    )):
        loads[name] = pltpu.make_async_copy(src, dst, load_sem.at[index])
        loads[name].start()

    pl.semaphore_wait(barrier, len(steady) + 2 * away.astype(jnp.int32))

    def gather(index, forest, halves, bufs):
        return Gather(p, forest, halves, bufs, local_sem.at[index], zsend.at[index], zrecv.at[index],
                      send.at[index], recv.at[index])

    lower, upper = pl.ds(0, 16), pl.ds(16, 16)
    q_gather = gather(0, SHALLOW, [weight_hbm.at[0, lower], weight_hbm.at[0, upper]], (qa, qb))
    kv_gather = gather(1, DEEP, None, (ka, kb))
    o_gather = gather(2, LAST, None, (None, ob))
    tokens = TpGather(p, hidden_hbm, hid, local_sem.at[2, 0], hsend, hrecv)
    placed = [
        pltpu.make_async_copy(weight_hbm.at[index, rows], place, local_sem.at[1, k])
        for k, (index, rows, place) in enumerate((
            (1, lower, kv_gather.own(0).at[0]), (1, upper, kv_gather.own(1).at[0]),
            (2, lower, kv_gather.own(1).at[1]), (2, upper, kv_gather.own(1).at[2]),
        ))
    ]
    for copy in placed:
        copy.start()
    q_gather.begin()
    for copy in placed:
        copy.wait()
    kv_gather.begin()
    tokens.begin()

    tx, ty, tz = lax.div(target_seq, 16), lax.rem(lax.div(target_seq, 2), NY), lax.rem(target_seq, 2)
    pieces = [out_weight_hbm.at[lower], out_weight_hbm.at[upper]]
    places = [ob.at[tx, ty, tz, k] for k in (0, 1)]
    moved = [remote(pieces[k], places[k], move_sem.at[k], move_sem.at[2 + k], target) for k in (0, 1)]
    stay = [pltpu.make_async_copy(pieces[k], places[k], move_sem.at[4 + k]) for k in (0, 1)]

    @pl.when(away)
    def _():
        for copy in moved:
            copy.start()

    @pl.when(jnp.logical_not(away))
    def _():
        for copy in stay:
            copy.start()

    q_gather.roots()

    length = length_ref[lax.div(p.s, 4)]
    first = local * SLOTS - length

    def aux(count, start, cached):
        place = lax.broadcasted_iota(jnp.int32, (count, HEAD_DIM), 0) + start
        lane = lax.broadcasted_iota(jnp.int32, (count, HEAD_DIM), 1)
        high = lax.shift_right_arithmetic(place, 7)
        low = place - high * 128
        number = jnp.where(lane < 3, high, jnp.where(lane < 6, low, 0)).astype(F32)
        if cached:
            number = jnp.where(place >= 0, jnp.where(lane == 6, -1e30, 0.0), number)
        return number.astype(BF16)

    def ones(count):
        return jnp.ones((count, HEAD_DIM), BF16)

    columns = [slice(0, HEAD_DIM), slice(HEAD_DIM, 2 * HEAD_DIM)]

    def prepare_keys():
        loads["keys"].wait()
        number = aux(SLOTS, first, True)
        alive = lax.broadcasted_iota(jnp.int32, (SLOTS, HEAD_DIM), 0) + first < 0
        for head in range(2):
            kaug[head, :, :HEAD_DIM] = jnp.where(alive, keys[:, columns[head]].astype(F32), 0.0).astype(BF16)
            kaug[head, :, HEAD_DIM:] = number

    def prepare_values():
        loads["values"].wait()
        for head in range(2):
            vaug[head, :, :HEAD_DIM] = values[:, columns[head]]
            vaug[head, :, HEAD_DIM:] = ones(SLOTS)

    def normalise(start, rows):
        numbers = [hid[t, start:start + rows, :].astype(F32) for t in range(TP)]
        mean = jnp.sum(functools.reduce(jnp.add, numbers), axis=1, keepdims=True) * (1.0 / (TP * ROWS))
        numbers = [v - mean for v in numbers]
        squares = functools.reduce(jnp.add, [v * v for v in numbers])
        variance = jnp.sum(squares, axis=1, keepdims=True) * (1.0 / (TP * ROWS))
        scale = lax.rsqrt(variance + 1e-05)
        for t in range(TP):
            cols = slice(t * ROWS, (t + 1) * ROWS)
            norm[t, start:start + rows, :] = (numbers[t] * scale * gain[:, cols] + shift[:, cols]).astype(BF16)

    def places(seqs):
        return [(q // (NY * NZ), (q // NZ) % NY, q % NZ) for q in seqs]

    def q_rows(seqs):
        return [ref for x, y, z in places(seqs) for ref in (qa[y, x, z], qb[x, y, z])]

    def k_rows(seqs):
        return [ref for x, y, z in places(seqs) for ref in (ka[y, x, z, 0], kb[x, y, z, 0])]

    def v_rows(seqs):
        return [ref for x, y, z in places(seqs) for ref in (kb[x, y, z, 1], kb[x, y, z, 2])]

    def out_rows(seqs):
        return [ref for x, y, z in places(seqs) for ref in (ob[x, y, z, 0], ob[x, y, z, 1])]

    def project(rows_of, row):
        total = None
        for t in range(TP):
            rows = jnp.concatenate(rows_of(range(t * 8, t * 8 + 8)), axis=0)
            part = jnp.dot(norm[t], rows, preferred_element_type=F32)
            total = part if total is None else total + part
        return total + bias[row:row + 1, :]

    prepare_keys()
    kv_gather.roots()
    q_gather.step(1)
    tokens.near()
    kv_gather.step(1)
    prepare_values()
    q_gather.step(2)
    tokens.far()
    kv_gather.step(2)
    q_gather.step(3)

    @pl.when(away)
    def _():
        for k in (0, 1):
            own = ob.at[p.x, p.y, p.z, k]
            remote(own, own, move_sem.at[k], move_sem.at[2 + k], source).wait_recv()
            moved[k].wait_send()

    @pl.when(jnp.logical_not(away))
    def _():
        for copy in stay:
            copy.wait()

    o_gather.begin()
    for name in ("gain", "shift", "bias", "out_bias", "table"):
        loads[name].wait()
    tokens.rest()
    normalise(0, 128)
    normalise(128, 128)
    queries[local] = (project(q_rows, 0) * (LOG2E / math.sqrt(HEAD_DIM))).astype(BF16)
    sent = []

    def exchange(src, dst, sems, index, peer):
        copy = remote(src, dst, sems[0].at[index], sems[1].at[index], peer)
        copy.start()
        sent.append(copy)

    def arrived(dst, sems, index, peer):
        remote(dst, dst, sems[0].at[index], sems[1].at[index], peer).wait_recv()

    for k in (1, 2, 3):
        exchange(queries.at[local], queries.at[local], (gsend, grecv), k, peers[k])

    def query_of(block, head):
        side = jnp.broadcast_to(table[head], (ROWS, HEAD_DIM)).astype(BF16)
        return jnp.concatenate([queries[block, :, columns[head]], side], axis=1)

    nt = (((1,), (1,)), ((), ()))

    def attend(k, block):
        for head in range(2):
            score = lax.dot_general(query_of(block, head), kaug[head], nt, preferred_element_type=F32)
            top = jnp.max(score, axis=1, keepdims=True)
            weight = jnp.exp2(score - top).astype(BF16)
            acc[2 * k + head] = jnp.dot(weight, vaug[head], preferred_element_type=F32)
            tops[2 * k + head] = jnp.broadcast_to(top, (ROWS, HEAD_DIM))

    blocks = [local] + [lax.rem(peer[0], 4) for peer in peers[1:]]
    kv_gather.step(3)
    attend(0, blocks[0])
    kv_gather.step(4)
    arrived(queries.at[blocks[1]], (gsend, grecv), 1, peers[1])
    attend(1, blocks[1])
    kv_gather.step(5)
    arrived(queries.at[blocks[2]], (gsend, grecv), 2, peers[2])
    attend(2, blocks[2])
    kv_gather.step(6)
    o_gather.roots()
    for which, rows_of in ((0, k_rows), (1, v_rows)):
        fresh_all[local, which] = project(rows_of, 1 + which).astype(BF16)
        if which == 0:
            exchange(fresh_all.at[local, 0], fresh_all.at[local, 0], (gsend, grecv), 4, peers[1])
            exchange(fresh_all.at[local, 0], fresh_all.at[local, 0], (gsend, grecv), 5, peers[2])
    number = aux(ROWS, local * ROWS, False)
    for head in range(2):
        kfresh[head, :, :HEAD_DIM] = fresh_all[local, 0, :, columns[head]]
        kfresh[head, :, HEAD_DIM:] = number
        vfresh[head, :, :HEAD_DIM] = fresh_all[local, 1, :, columns[head]]
        vfresh[head, :, HEAD_DIM:] = ones(ROWS)

    def attend_fresh(k, block, put_part, put_side):
        row = lax.broadcasted_iota(jnp.int32, (ROWS, ROWS), 0) + block * ROWS
        column = lax.broadcasted_iota(jnp.int32, (ROWS, ROWS), 1) + local * ROWS
        lses = []
        for head in range(2):
            score = lax.dot_general(query_of(block, head), kfresh[head], nt, preferred_element_type=F32)
            score = jnp.where(column <= row, score, -1e30)
            before = tops[2 * k + head]
            top = jnp.maximum(before, jnp.max(score, axis=1, keepdims=True))
            weight = jnp.exp2(score - jnp.concatenate([top, top], axis=1)).astype(BF16)
            keep = jnp.exp2(before - top)
            both = jnp.dot(weight, vfresh[head], preferred_element_type=F32)
            number = both[:, :HEAD_DIM] + acc[2 * k + head, :, :HEAD_DIM] * keep
            total = both[:, HEAD_DIM:] + acc[2 * k + head, :, HEAD_DIM:] * keep
            put_part(columns[head], (number / total).astype(BF16))
            lses.append(top + jnp.log2(total))
        lane = lax.broadcasted_iota(jnp.int32, (ROWS, HEAD_DIM), 1)
        put_side(jnp.transpose(jnp.where(lane == 0, lses[0], lses[1]))[:8])

    def put(ref, index):
        def store(cols, value):
            ref[index, :, cols] = value
        return store

    def put_all(ref, index):
        def store(value):
            ref[index] = value
        return store

    def send_part(k):
        exchange(part_out.at[k], parts.at[local], (psend, precv), k, peers[k])
        exchange(side_out.at[k], sides.at[local], (psend, precv), 4 + k, peers[k])

    attend_fresh(1, blocks[1], put(part_out, 1), put_all(side_out, 1))
    attend_fresh(2, blocks[2], put(part_out, 2), put_all(side_out, 2))
    send_part(1)
    arrived(queries.at[blocks[3]], (gsend, grecv), 3, peers[3])
    send_part(2)
    attend(3, blocks[3])
    attend_fresh(3, blocks[3], put(part_out, 3), put_all(side_out, 3))
    attend_fresh(0, blocks[0], put(parts, local), put_all(sides, local))
    send_part(3)
    exchange(fresh_all.at[local, 1], fresh_all.at[local, 1], (gsend, grecv), 6, peers[1])
    exchange(fresh_all.at[local, 1], fresh_all.at[local, 1], (gsend, grecv), 7, peers[2])
    key_block = fresh_all.at[blocks[1], 0]
    arrived(key_block, (gsend, grecv), 4, peers[1])
    exchange(key_block, key_block, (gsend, grecv), 8, peers[2])
    o_gather.step(1)
    for k in (1, 2, 3):
        arrived(parts.at[blocks[k]], (psend, precv), k, peers[k])
        arrived(sides.at[blocks[k]], (psend, precv), 4 + k, peers[k])
    stats = [sides[k] for k in range(4)]
    top = functools.reduce(jnp.maximum, stats)
    shares = [jnp.exp2(stat - top) for stat in stats]
    total = functools.reduce(jnp.add, shares)
    shares = [jnp.transpose(jnp.concatenate([share / total] * 16, axis=0)) for share in shares]
    for head in range(2):
        terms = [parts[k, :, columns[head]].astype(F32) * shares[k][:, head:head + 1] for k in range(4)]
        mine[:, columns[head]] = functools.reduce(jnp.add, terms).astype(BF16)
    tokens.finish()
    finals = TpGather(p, mine, att, local_sem.at[2, 1], tsend, trecv)
    finals.begin()
    for k in range(2):
        for h in range(2):
            fresh[2 * k + h, :PAD] = jnp.zeros((PAD, HEAD_DIM), F32)
            fresh[2 * k + h, PAD + SPAN:] = jnp.zeros((PAD, HEAD_DIM), F32)
    finals.near()
    o_gather.step(2)
    value_block = fresh_all.at[blocks[1], 1]
    arrived(value_block, (gsend, grecv), 6, peers[1])
    exchange(value_block, value_block, (gsend, grecv), 9, peers[2])
    finals.far()
    arrived(fresh_all.at[blocks[2], 0], (gsend, grecv), 5, peers[2])
    arrived(fresh_all.at[blocks[2], 1], (gsend, grecv), 7, peers[2])
    arrived(fresh_all.at[blocks[3], 0], (gsend, grecv), 8, peers[2])
    arrived(fresh_all.at[blocks[3], 1], (gsend, grecv), 9, peers[2])
    stores = []
    for k, (rows_of, out) in enumerate(((keys, keys_out), (values, values_out))):
        for h in range(2):
            for block in range(4):
                begin = PAD + block * ROWS
                fresh[2 * k + h, begin:begin + ROWS] = fresh_all[block, k, :, columns[h]].astype(F32)

        for chunk in range(SLOTS // ROWS):
            begin = jnp.clip(first + chunk * ROWS, -ROWS, SPAN)
            place = lax.broadcasted_iota(jnp.int32, (ROWS, HEAD_DIM), 0) + begin
            inside = (place >= 0) & (place < SPAN)
            span = slice(chunk * ROWS, (chunk + 1) * ROWS)
            for h in range(2):
                new = fresh[2 * k + h, pl.ds(begin + PAD, ROWS), :]
                old = rows_of[span, columns[h]].astype(F32)
                rows_of[span, columns[h]] = jnp.where(inside, new, old).astype(BF16)
        stores.append(pltpu.make_async_copy(rows_of, out, load_sem.at[7 + k]))
        stores[-1].start()
    o_gather.step(3)
    finals.rest()

    result = None
    for t in range(TP):
        rows = jnp.concatenate(out_rows(range(t, 64, TP)), axis=0)
        term = lax.dot_general(att[t], rows, nt, preferred_element_type=F32)
        result = term if result is None else result + term
    out_ref[...] = (result + out_bias[...]).astype(BF16)
    for copy in stores:
        copy.wait()
    for copy in sent:
        copy.wait_send()
    for who in (q_gather, kv_gather, o_gather, finals):
        who.finish()


def hand_over_kernel(mixed, keys, values, mixed_out, keys_out, values_out, a, b, c, in_sem, out_sem):
    copies = []
    for src, mid, dst, count in ((mixed, a, mixed_out, 1), (keys, b, keys_out, 4), (values, c, values_out, 4)):
        rows = src.shape[0] // count
        for k in range(count):
            span = pl.ds(k * rows, rows)
            index = len(copies)
            copies.append((
                pltpu.make_async_copy(src.at[span], mid.at[span], in_sem.at[index]),
                pltpu.make_async_copy(mid.at[span], dst.at[span], out_sem.at[index]),
            ))
    for first, _ in copies:
        first.start()
    for first, second in copies:
        first.wait()
        second.start()
    for _, second in copies:
        second.wait()


def round_bf16(value):
    return np.asarray(np.asarray(value, np.float32).astype(jnp.bfloat16), np.float64)


def bias_table():
    table = np.zeros((HEADS, 1, HEAD_DIM), np.float64)
    for head in range(HEADS):
        slope = 2.0 ** (-8.0 * (head + 1) / HEADS) * LOG2E
        for column, value in ((0, slope * 128.0), (3, slope)):
            rest = value
            for k in range(3):
                table[head, 0, column + k] = round_bf16(rest)
                rest = rest - table[head, 0, column + k]
        table[head, 0, 6] = 1.0
    return table.astype(np.float32)


def dma(*count):
    return pltpu.SemaphoreType.DMA(count)


def on_device(
    hidden_in, norm_gain, norm_bias, qkv_weight, qkv_bias, out_weight, out_bias, key_cache, value_cache, cached_len,
):
    any_spec = pl.BlockSpec(memory_space=pl.ANY)

    def vm(*shape, dtype=BF16):
        return pltpu.VMEM(shape, dtype)

    results = pl.pallas_call(
        layer_kernel,
        name="layer",
        out_shape=(
            jax.ShapeDtypeStruct((ROWS, ROWS), BF16),
            jax.ShapeDtypeStruct((SLOTS, ROWS), BF16),
            jax.ShapeDtypeStruct((SLOTS, ROWS), BF16),
        ),
        in_specs=[SMEM_SPEC] + [any_spec] * 10,
        out_specs=(VMEM_SPEC, any_spec, any_spec),
        scratch_shapes=[
            vm(4, 2, ROWS, ROWS), vm(4, SPAN + 2 * PAD, HEAD_DIM, dtype=F32),
            vm(TP, ROWS, ROWS), vm(TP, ROWS, ROWS),
            vm(NY, NX, NZ, 16, ROWS), vm(NX, NY, NZ, 16, ROWS),
            vm(NY, NX, NZ, 1, 16, ROWS), vm(NX, NY, NZ, 3, 16, ROWS), vm(NX, NY, NZ, 2, 16, ROWS),
            vm(1, TP * ROWS, dtype=F32), vm(1, TP * ROWS, dtype=F32), vm(3, ROWS, dtype=F32), vm(1, ROWS, dtype=F32),
            vm(2, 1, HEAD_DIM, dtype=F32), vm(SLOTS, ROWS), vm(SLOTS, ROWS),
            vm(2, SLOTS, ROWS), vm(2, SLOTS, ROWS), vm(2, ROWS, ROWS), vm(2, ROWS, ROWS),
            vm(4, ROWS, ROWS), vm(8, ROWS, ROWS, dtype=F32), vm(8, ROWS, HEAD_DIM, dtype=F32),
            vm(4, ROWS, ROWS), vm(4, 8, ROWS, dtype=F32), vm(4, ROWS, ROWS), vm(4, 8, ROWS, dtype=F32),
            vm(ROWS, ROWS), vm(TP, ROWS, ROWS),
            dma(9), dma(3, 4), dma(6), dma(3, 2), dma(3, 2), dma(3, N_EDGES), dma(3, N_EDGES),
            dma(10), dma(10), dma(10), dma(10), dma(8), dma(8), dma(10), dma(10),
        ],
        compiler_params=pltpu.CompilerParams(collective_id=0, has_side_effects=True, vmem_limit_bytes=56 << 20),
    )(
        cached_len, hidden_in, norm_gain.reshape(1, TP * ROWS), norm_bias.reshape(1, TP * ROWS),
        qkv_weight, qkv_bias, out_weight.T, out_bias.reshape(1, ROWS), key_cache, value_cache,
        jnp.asarray(bias_table()),
    )
    return pl.pallas_call(
        hand_over_kernel,
        name="hand_over",
        out_shape=tuple(jax.ShapeDtypeStruct(r.shape, r.dtype) for r in results),
        in_specs=[any_spec] * 3,
        out_specs=(any_spec,) * 3,
        scratch_shapes=[vm(ROWS, ROWS), vm(SLOTS, ROWS), vm(SLOTS, ROWS), dma(9), dma(9)],
    )(*results)


def solution(mesh):
    placed = (
        P("seq", "tp"),
        P(),
        P(),
        P(None, "seq", "tp"),
        P(None, "tp"),
        P("tp", "seq"),
        P("tp"),
        P("seq", "tp"),
        P("seq", "tp"),
        P(),
    )
    return jax.shard_map(
        on_device,
        mesh=mesh,
        in_specs=placed,
        out_specs=(P("seq", "tp"), P("seq", "tp"), P("seq", "tp")),
        check_vma=False,
    )
```
